32 devices in a mesh: tp: 4 (over y, x), grp: 8 (over z, core).
Axes of the slice: x: 2, y: 2, z: 4, core: 2. Of those that a mesh axis runs over, the one named last changes fastest.
Arguments:
- low_feats: bfloat16 [384, 16384], P('grp', 'tp'), may hold values from -40 to 40
- mid_feats: bfloat16 [384, 16384], P('grp', 'tp'), may hold values from -40 to 40
- high_feats: bfloat16 [384, 16384], P('grp', 'tp'), may hold values from -40 to 40
- w_low: bfloat16 [16384, 16384], P('tp', 'grp'), may hold values from -3 to 3
- w_mid: bfloat16 [16384, 16384], P('tp', 'grp'), may hold values from -3 to 3
- w_high: bfloat16 [16384, 16384], P('tp', 'grp'), may hold values from -3 to 3
- norm_gain: float32 [16384], P('grp'), may hold values from 0.1 to 1.9
- accepted: int32 [64], replicated, may hold values from 0 to 5, as said below
- assignment: int32 [64], replicated, may hold values from 0 to 63, each once
Outputs:
- drafted: bfloat16 [384, 16384], P('tp', 'grp')
The draws below stay inside these ranges and needn't reach their ends.
Inputs may be any that keep to these rules, and one draw needn't show every extreme that they name: For every group of 8 consecutive rows starting at a multiple of 8, the sum of accepted + 1 is at most 32, and some group reaches 32; rows 2i and 2i+1 together have at most 8 positions with p <= accepted. `assignment`: each row appears once.
All inputs are finite; a program needn't handle non-finite values.
Results may differ from the reference program's by a relative error of at most 0.0008.
Values may be sent and summed in bfloat16 or wider, within the bound.
A program may use at most 128 MiB of HBM per device.

```python
import math
import jax
import jax.numpy as jnp
from jax import lax

D = 16384
ROWS_G = 8
POS = 6
ROWS = 64
TOKENS = 384


def feature_draw(key):
    key_rows, key_vals = jax.random.split(key, 2)
    row_scale = jnp.exp(jax.random.uniform(key_rows, (TOKENS, 1), jnp.float32, 0.0, math.log(10.0)))
    values = jax.random.normal(key_vals, (TOKENS, D), jnp.float32)
    values = jnp.clip(values, -4.0, 4.0)
    return (values * row_scale).astype(jnp.bfloat16)


def weight_draw(key):
    key_cols, key_vals = jax.random.split(key, 2)
    columns = jnp.arange(D, dtype=jnp.float32)
    col_scale = jnp.exp(math.log(3.0) * columns / D)[None, :]
    col_scale = col_scale * jnp.exp(jax.random.uniform(key_cols, (1, D), jnp.float32, 0.0, math.log(3.3)))
    values = jnp.clip(jax.random.normal(key_vals, (D, D), jnp.float32), -4.0, 4.0)
    return (values * col_scale * (0.5 / math.sqrt(D))).astype(jnp.bfloat16)


def draw_low_feats(key, part):
    return feature_draw(jax.random.fold_in(key, 11))


def draw_mid_feats(key, part):
    return feature_draw(jax.random.fold_in(key, 12))


def draw_high_feats(key, part):
    return feature_draw(jax.random.fold_in(key, 13))


def draw_w_low(key, part):
    return weight_draw(jax.random.fold_in(key, 21))


def draw_w_mid(key, part):
    return weight_draw(jax.random.fold_in(key, 22))


def draw_w_high(key, part):
    return weight_draw(jax.random.fold_in(key, 23))


def draw_accepted(key, part):
    key_upper, key_full, key_sums, key_split = jax.random.split(jax.random.fold_in(key, 31), 4)
    groups = ROWS // ROWS_G
    pairs = ROWS_G // 2
    group_index = jnp.arange(groups, dtype=jnp.int32)[:, None]
    upper = jax.random.randint(key_upper, (groups, 1), 2, 9)
    full_group = jax.random.randint(key_full, (), 0, groups)
    upper = jnp.where(group_index == full_group, 8, upper)
    lower = jnp.where(group_index == full_group, 8, 2)
    pair_sum = jax.random.randint(key_sums, (groups, pairs), lower, upper + 1)
    first_low = jnp.maximum(1, pair_sum - 6)
    first_high = jnp.minimum(6, pair_sum - 1)
    raw_bits = jax.random.randint(key_split, (groups, pairs), 0, 1 << 20)
    first = first_low + raw_bits % (first_high - first_low + 1)
    second = pair_sum - first
    used = jnp.stack([first, second], axis=-1).reshape(ROWS)
    return (used - 1).astype(jnp.int32)


def setup_inputs(seed: int = 0) -> dict:
    key_list = jax.random.split(jax.random.key(seed), 10)
    low_feats = draw_low_feats(jax.random.fold_in(key_list[9], 71), 0)
    mid_feats = draw_mid_feats(jax.random.fold_in(key_list[9], 71), 0)
    high_feats = draw_high_feats(jax.random.fold_in(key_list[9], 71), 0)
    w_low = draw_w_low(jax.random.fold_in(key_list[9], 71), 0)
    w_mid = draw_w_mid(jax.random.fold_in(key_list[9], 71), 0)
    w_high = draw_w_high(jax.random.fold_in(key_list[9], 71), 0)
    norm_gain = jnp.clip(1.0 + 0.18 * jax.random.normal(key_list[6], (D,), jnp.float32), 0.1, 1.9)
    accepted = draw_accepted(jax.random.fold_in(key_list[9], 71), 0)
    assignment = jax.random.permutation(key_list[8], ROWS).astype(jnp.int32)
    return dict(low_feats=low_feats, mid_feats=mid_feats, high_feats=high_feats, w_low=w_low, w_mid=w_mid, w_high=w_high, norm_gain=norm_gain, accepted=accepted, assignment=assignment)


EPSILON = 1e-05

def reference(low_feats, mid_feats, high_feats, w_low, w_mid, w_high, norm_gain, accepted, assignment):
    joined_rows = jnp.dot(low_feats, w_low, preferred_element_type=jnp.float32)
    joined_rows = joined_rows + jnp.dot(mid_feats, w_mid, preferred_element_type=jnp.float32)
    joined_rows = joined_rows + jnp.dot(high_feats, w_high, preferred_element_type=jnp.float32)
    total_tokens = accepted.shape[0] * POS
    step_index = jnp.arange(POS, dtype=jnp.int32)
    source_rows = (assignment[:, None] * POS + step_index[None, :]).reshape(total_tokens).astype(jnp.int32)
    live_rows = (step_index[None, :] <= accepted[assignment][:, None]).reshape(total_tokens)
    ordered = joined_rows[source_rows]
    squares = lax.optimization_barrier(jnp.sum(ordered * ordered, axis=1, keepdims=True))
    normed = ordered * lax.rsqrt(squares / D + EPSILON) * norm_gain[None, :]
    return jnp.where(live_rows[:, None], normed, jnp.zeros_like(normed)).astype(jnp.bfloat16)
```

```python
import functools

import jax
import jax.numpy as jnp
from jax import lax
from jax.experimental import pallas as pl
from jax.experimental.pallas import tpu as pltpu
from jax.sharding import PartitionSpec as P

ROWS_G = 8
POS = 6
CAPACITY = 4 * ROWS_G
BATCHES = 2
SLOTS = CAPACITY // BATCHES
LAYERS = 3
STEPS = BATCHES * LAYERS
AHEAD = 2
TILE = 256
PIECES = 1
EPSILON = 1e-05


def kernel(
    groups, owners,
    low_ref, mid_ref, high_ref, w_low, w_mid, w_high, gain_ref, accepted_ref, assignment_ref,
    out_ref,
    feats, weights, blocks, sums, parts, squares, rows_out, pick,
    f_sem, w_sem, send_sem, recv_sem, part_send, part_recv, sq_send, sq_recv, row_send, row_recv,
):
    me = lax.axis_index("grp")
    own = lax.axis_index("tp")
    chip, core = me // 2, me % 2
    chips = groups // 2
    sibling = chip * 2 + 1 - core
    columns = sums.shape[2]
    share = rows_out.shape[2]
    width = groups * columns
    tiles = columns // TILE
    tokens = feats.shape[1]
    slab = out_ref.shape[0]
    pair_slots = 2 * CAPACITY // ROWS_G

    reads = [
        pltpu.make_async_copy(f, feats.at[i], f_sem.at[i])
        for i, f in enumerate((low_ref, mid_ref, high_ref))
    ]
    for read in reads:
        read.start()
    loads = [
        pltpu.make_async_copy(w, weights.at[i], w_sem.at[i])
        for i, w in enumerate((w_low, w_mid, w_high))
    ]

    barrier = pltpu.get_barrier_semaphore()
    for d in range(1, groups):
        pl.semaphore_signal(
            barrier, inc=1, device_id={"grp": lax.rem(me + d, groups)},
            device_id_type=pl.DeviceIdType.MESH,
        )
    for d in range(1, owners):
        pl.semaphore_signal(
            barrier, inc=1, device_id={"tp": lax.rem(own + d, owners)},
            device_id_type=pl.DeviceIdType.MESH,
        )

    def rows_of(group):
        return pl.ds(pl.multiple_of(group * SLOTS, SLOTS), SLOTS)

    slot = lax.broadcasted_iota(jnp.int32, (CAPACITY, tokens), 0)
    token = lax.broadcasted_iota(jnp.int32, (CAPACITY, tokens), 1)
    packing = jnp.zeros((CAPACITY, tokens), jnp.float32)
    for k in range(ROWS_G):
        count = accepted_ref[me * ROWS_G + k] + 1
        start = (k // 2) * pair_slots
        if k % 2 == 1:
            start = start + accepted_ref[me * ROWS_G + k - 1] + 1
        position = token - k * POS
        hit = (position >= 0) & (position < count) & (slot == start + position)
        packing = jnp.where(hit, 1.0, packing)
    packing = packing.astype(jnp.bfloat16)

    def pack(layer):
        reads[layer].wait()
        packed = jnp.dot(packing, feats[layer], preferred_element_type=jnp.float32)
        for b in range(BATCHES):
            blocks[b * LAYERS + layer, rows_of(me), :] = packed[
                b * SLOTS : (b + 1) * SLOTS
            ].astype(jnp.bfloat16)

    pack(0)
    pl.semaphore_wait(barrier, groups + owners - 2)

    def block_copy(way, step, group):
        target = (chip * 2 + 2 + core, chip * 2 - 2 + core, sibling)[way]
        return pltpu.make_async_remote_copy(
            src_ref=blocks.at[step, rows_of(group), :],
            dst_ref=blocks.at[step, rows_of(group), :],
            send_sem=send_sem.at[way, step, group // 2],
            recv_sem=recv_sem.at[step, group],
            device_id={"grp": target},
            device_id_type=pl.DeviceIdType.MESH,
        )

    def send_own(step):
        @pl.when(chip < chips - 1)
        def _():
            block_copy(0, step, me).start()

        @pl.when(chip > 0)
        def _():
            block_copy(1, step, me).start()

        block_copy(2, step, me).start()

    def relay(step, d):
        @pl.when(chip - d >= 0)
        def _():
            group = me - 2 * d
            block_copy(0, step, group).wait_recv()

            @pl.when(chip < chips - 1)
            def _():
                block_copy(0, step, group).start()

            block_copy(2, step, group).start()

        @pl.when(chip + d <= chips - 1)
        def _():
            group = me + 2 * d
            block_copy(1, step, group).wait_recv()

            @pl.when(chip > 0)
            def _():
                block_copy(1, step, group).start()

            block_copy(2, step, group).start()

    def relays(step, first, last):
        @pl.loop(first, last)
        def _(d):
            relay(step, d)

    def arrive(step):
        for q in range(chips):
            block_copy(2, step, q * 2 + 1 - core).wait_recv()

    def multiply(step):
        b, layer = step // LAYERS, step % LAYERS

        @pl.loop(0, tiles)
        def _(j):
            cols = pl.ds(pl.multiple_of(j * TILE, TILE), TILE)
            product = jnp.dot(
                blocks[step], weights[layer, :, cols], preferred_element_type=jnp.float32
            )
            if layer == 0:
                sums[b, :, cols] = product
            else:
                sums[b, :, cols] += product
            if layer == LAYERS - 1:
                @pl.when(j % piece_tiles == piece_tiles - 1)
                def _():
                    for d in range(1, owners):
                        part_copy(b, d, j // piece_tiles).start()

            if step + 1 < STEPS:
                relays(
                    step + 1,
                    1 + (chips - 1) * j // tiles,
                    1 + (chips - 1) * (j + 1) // tiles,
                )
            if b > 0 and layer == 1:
                @pl.when(j == tiles // 2)
                def _():
                    reduce(b - 1)

    def share_of(owner):
        return pl.ds(pl.multiple_of(owner * share, share), share)

    piece = columns // PIECES
    piece_tiles = tiles // PIECES

    def part_copy(b, d, h):
        cols = pl.ds(pl.multiple_of(h * piece, piece), piece)
        target = lax.rem(own + d, owners)
        return pltpu.make_async_remote_copy(
            src_ref=sums.at[b, share_of(target), cols],
            dst_ref=parts.at[b, d - 1, :, cols],
            send_sem=part_send.at[b, d - 1, h],
            recv_sem=part_recv.at[b, d - 1, h],
            device_id={"tp": target},
            device_id_type=pl.DeviceIdType.MESH,
        )

    def square_copy(b, d):
        return pltpu.make_async_remote_copy(
            src_ref=squares.at[b, 0],
            dst_ref=squares.at[b, d],
            send_sem=sq_send.at[b, d - 1],
            recv_sem=sq_recv.at[b, d - 1],
            device_id={"grp": lax.rem(me + d, groups)},
            device_id_type=pl.DeviceIdType.MESH,
        )

    def row_copy(b, d):
        return pltpu.make_async_remote_copy(
            src_ref=rows_out.at[b, own],
            dst_ref=rows_out.at[b, own],
            send_sem=row_send.at[b, d - 1],
            recv_sem=row_recv.at[b, d - 1],
            device_id={"tp": lax.rem(own + d, owners)},
            device_id_type=pl.DeviceIdType.MESH,
        )

    diagonal = lax.broadcasted_iota(jnp.int32, (share, 128), 0) == lax.broadcasted_iota(
        jnp.int32, (share, 128), 1
    )

    def reduce(b):
        def body(h, square):
            cols = pl.ds(pl.multiple_of(h * piece, piece), piece)
            total = sums[b, share_of(own), cols]
            for d in range(1, owners):
                part_copy(b, d, h).wait_recv()
                total = total + parts[b, d - 1, :, cols]
            parts[b, owners - 1, :, cols] = total
            return square + jnp.sum(total * total, axis=1, keepdims=True)

        square = lax.fori_loop(0, PIECES, body, jnp.zeros((share, 1), jnp.float32))
        lanes = jnp.sum(jnp.where(diagonal, square, 0.0), axis=0, keepdims=True)
        squares[b, 0] = jnp.broadcast_to(lanes, (8, 128))
        for d in range(1, groups):
            square_copy(b, d).start()

    def finish(b):
        for d in range(1, groups):
            square_copy(b, d).wait_recv()
        lanes = squares[b, 0]
        for d in range(1, groups):
            lanes = lanes + squares[b, d]
        square = jnp.sum(jnp.where(diagonal, lanes[0:1], 0.0), axis=1, keepdims=True)
        inverse = lax.rsqrt(square / width + EPSILON)
        rows_out[b, own] = (parts[b, owners - 1] * inverse * gain_ref[...]).astype(jnp.bfloat16)
        for d in range(1, owners):
            row_copy(b, d).start()

    send_own(0)
    pack(1)
    send_own(1)
    for load in loads:
        load.start()
    pack(2)

    column = lax.broadcasted_iota(jnp.int32, pick.shape, 1)
    batch_rows = groups * SLOTS
    batch_bits, slot_bits = batch_rows.bit_length() - 1, SLOTS.bit_length() - 1
    group_of = lax.shift_right_logical(column & (batch_rows - 1), slot_bits)
    slot_of = lax.shift_right_logical(column, batch_bits) * SLOTS + (column & (SLOTS - 1))
    place = group_of * CAPACITY + slot_of
    line = lax.broadcasted_iota(jnp.int32, pick.shape, 0)
    picking = jnp.zeros(pick.shape, jnp.float32)
    for k in range(slab // POS):
        source = assignment_ref[own * (slab // POS) + k]
        count = accepted_ref[source] + 1
        local = source & (ROWS_G - 1)
        odd = local & 1
        before = (accepted_ref[jnp.maximum(source - 1, 0)] + 1) * odd
        start = (source - local) // ROWS_G * CAPACITY + (local - odd) // 2 * pair_slots + before
        position = line - k * POS
        hit = (position >= 0) & (position < count) & (place == start + position)
        picking = jnp.where(hit, 1.0, picking)
    pick[...] = picking.astype(jnp.bfloat16)

    relays(0, 1, chips)
    arrive(0)
    for step in range(STEPS):
        if step + AHEAD < STEPS:
            send_own(step + AHEAD)
        if step < LAYERS:
            loads[step].wait()
        multiply(step)
        if step + 1 < STEPS:
            arrive(step + 1)
        if step >= LAYERS and step % LAYERS == 2:
            finish(step // LAYERS - 1)
    reduce(BATCHES - 1)
    finish(BATCHES - 1)
    for b in range(BATCHES):
        for d in range(1, owners):
            row_copy(b, d).wait_recv()

    everything = rows_out[...].reshape(BATCHES * owners * share, columns)
    out_ref[...] = jnp.dot(
        pick[...], everything, preferred_element_type=jnp.float32
    ).astype(jnp.bfloat16)

    for step in range(STEPS):
        for q in range(chips):
            group = q * 2 + core

            @pl.when((chip < chips - 1) & (q <= chip))
            def _():
                block_copy(0, step, group).wait_send()

            @pl.when((chip > 0) & (q >= chip))
            def _():
                block_copy(1, step, group).wait_send()

            block_copy(2, step, group).wait_send()
    for b in range(BATCHES):
        for d in range(1, owners):
            for h in range(PIECES):
                part_copy(b, d, h).wait_send()
            row_copy(b, d).wait_send()
        for d in range(1, groups):
            square_copy(b, d).wait_send()


def full_call(
    groups, owners,
    low_feats, mid_feats, high_feats, w_low, w_mid, w_high, norm_gain, accepted, assignment,
):
    tokens, depth = low_feats.shape
    columns = w_low.shape[1]
    rows = accepted.shape[0]
    batch_rows = groups * SLOTS
    share = batch_rows // owners
    slab = rows * POS // owners

    vmem = pl.BlockSpec(memory_space=pltpu.VMEM)
    hbm = pl.BlockSpec(memory_space=pl.ANY)
    smem = pl.BlockSpec(memory_space=pltpu.SMEM)
    dma = pltpu.SemaphoreType.DMA
    return pl.pallas_call(
        functools.partial(kernel, groups, owners),
        out_shape=jax.ShapeDtypeStruct((slab, columns), jnp.bfloat16),
        in_specs=[hbm] * 6 + [vmem] + [smem] * 2,
        out_specs=vmem,
        scratch_shapes=[
            pltpu.VMEM((LAYERS, tokens, depth), jnp.bfloat16),
            pltpu.VMEM((LAYERS, depth, columns), jnp.bfloat16),
            pltpu.VMEM((STEPS, batch_rows, depth), jnp.bfloat16),
            pltpu.VMEM((BATCHES, batch_rows, columns), jnp.float32),
            pltpu.VMEM((BATCHES, owners, share, columns), jnp.float32),
            pltpu.VMEM((BATCHES, groups, 8, 128), jnp.float32),
            pltpu.VMEM((BATCHES, owners, share, columns), jnp.bfloat16),
            pltpu.VMEM((slab, BATCHES * batch_rows), jnp.bfloat16),
            dma((LAYERS,)),
            dma((LAYERS,)),
            dma((3, STEPS, groups // 2)),
            dma((STEPS, groups)),
            dma((BATCHES, owners - 1, PIECES)),
            dma((BATCHES, owners - 1, PIECES)),
            dma((BATCHES, groups - 1)),
            dma((BATCHES, groups - 1)),
            dma((BATCHES, owners - 1)),
            dma((BATCHES, owners - 1)),
        ],
        compiler_params=pltpu.CompilerParams(
            collective_id=0, has_side_effects=True, vmem_limit_bytes=67043328
        ),
    )(low_feats, mid_feats, high_feats, w_low, w_mid, w_high, norm_gain[None, :], accepted, assignment)


CHUNK = 512
PIECE = 512


def fast_kernel(
    groups, owners, hop, room,
    low_ref, mid_ref, high_ref, w_low, w_mid, w_high, gain_ref, accepted_ref, assignment_ref,
    out_ref,
    lines, tokens_in, weights, joined, sums, parts, squares, slots, place, spread, before,
    raw_sem, near_sem, near_send, w_sem, hop_send, hop_recv, pair_send, pair_recv,
    part_send, part_recv, sq_send, sq_recv,
):
    me = lax.axis_index("grp")
    own = lax.axis_index("tp")
    chip, core = me // 2, me % 2
    chips = groups // 2
    last = chips - 1
    sibling = chip * 2 + 1 - core
    feats = (low_ref, mid_ref, high_ref)
    tokens, depth = low_ref.shape
    pieces, _, piece = sums.shape
    columns = pieces * piece
    half = depth // 2
    chunk = joined.shape[3]
    per_layer = half // chunk
    chunks = LAYERS * per_layer
    rows = accepted_ref.shape[0]
    slab = out_ref.shape[0]
    row_slots = slab // POS
    chip_rows = 2 * ROWS_G
    raw = 2 * tokens
    width = groups * columns
    mesh_id = pl.DeviceIdType.MESH

    barrier = pltpu.get_barrier_semaphore()
    for d in range(1, groups):
        pl.semaphore_signal(
            barrier, inc=1, device_id={"grp": lax.rem(me + d, groups)}, device_id_type=mesh_id
        )
    for d in range(1, owners):
        pl.semaphore_signal(
            barrier, inc=1, device_id={"tp": lax.rem(own + d, owners)}, device_id_type=mesh_id
        )

    def feature_cols(which, part):
        return pl.ds(pl.multiple_of(which * half + part * chunk, chunk), chunk)

    def own_read(f, k):
        return pltpu.make_async_copy(
            f.at[:, feature_cols(core, k % per_layer)], tokens_in.at[k, core], raw_sem.at[k]
        )

    def near_copy(f, k, side):
        return pltpu.make_async_remote_copy(
            src_ref=f.at[:, feature_cols(1 - core, k % per_layer)],
            dst_ref=tokens_in.at[k, side],
            send_sem=near_send.at[k],
            recv_sem=near_sem.at[k],
            device_id={"grp": sibling},
            device_id_type=mesh_id,
        )

    for k in range(chunks):
        own_read(feats[k // per_layer], k).start()

    def weight_copy(k, side):
        which = core + side - 2 * core * side
        at = pl.ds(pl.multiple_of(which * half + k % per_layer * chunk, chunk), chunk)
        return pltpu.make_async_copy(
            (w_low, w_mid, w_high)[k // per_layer].at[at, :], weights.at[k, side], w_sem.at[k, side]
        )

    for k in range(chunks):
        for side in range(2):
            weight_copy(k, side).start()

    def count_row(r, total):
        before[r] = total
        return total + accepted_ref[r] + 1

    total = lax.fori_loop(0, rows, count_row, jnp.int32(0))

    token = lax.broadcasted_iota(jnp.int32, (1, raw), 1)
    slot = jnp.full((1, raw), -1, jnp.int32)
    for k in range(chip_rows):
        r = chip * chip_rows + k
        position = token - k * POS
        hit = (position >= 0) & (position <= accepted_ref[r])
        slot = jnp.where(hit, before[r] + position, slot)
    line = lax.broadcasted_iota(jnp.int32, (hop, raw), 0)
    slots[0] = jnp.where(line == slot, 1.0, 0.0).astype(jnp.bfloat16)
    from_end = jnp.where(slot >= 0, slot + (hop - total), -1)
    slots[1] = jnp.where(line == from_end, 1.0, 0.0).astype(jnp.bfloat16)

    lane = lax.broadcasted_iota(jnp.int32, (1, 2 * hop + raw), 1)

    def place_row(j, carry):
        dest, used = carry
        used = jnp.where(j % row_slots == 0, 0, used)
        r = assignment_ref[j]
        first = before[r]
        local = r - chip * chip_rows
        start = jnp.where(
            local < 0,
            first,
            jnp.where(local < chip_rows, hop + local * POS, hop + raw + hop - total + first),
        )
        position = lane - start
        hit = (position >= 0) & (position <= accepted_ref[r])
        dest = jnp.where(hit, j // row_slots * room + used + position, dest)
        return dest, used + accepted_ref[r] + 1

    dest, _ = lax.fori_loop(
        0, rows, place_row, (jnp.full(lane.shape, -1, jnp.int32), jnp.int32(0))
    )
    line = lax.broadcasted_iota(jnp.int32, place.shape, 0)
    place[...] = jnp.where(line == dest, 1.0, 0.0).astype(jnp.bfloat16)

    line = lax.broadcasted_iota(jnp.int32, spread.shape, 0)
    column = lax.broadcasted_iota(jnp.int32, spread.shape, 1)
    spreading = jnp.zeros(spread.shape, jnp.float32)
    used = jnp.int32(0)
    for k in range(row_slots):
        more = accepted_ref[assignment_ref[own * row_slots + k]]
        position = line - k * POS
        hit = (position >= 0) & (position <= more) & (column == used + position)
        spreading = jnp.where(hit, 1.0, spreading)
        used = used + more + 1
    spread[...] = spreading.astype(jnp.bfloat16)

    pl.semaphore_wait(barrier, groups + owners - 2)
    for k in range(chunks):
        near_copy(feats[k // per_layer], k, core).start()

    def stream_copy(way, k):
        return pltpu.make_async_remote_copy(
            src_ref=lines.at[k, way],
            dst_ref=lines.at[k, way],
            send_sem=hop_send.at[way, k],
            recv_sem=hop_recv.at[way, k],
            device_id={"grp": (me + 2, me - 2)[way]},
            device_id_type=mesh_id,
        )

    def passes_on(way):
        return (chip < last, chip > 0)[way]

    def here(k):
        return tokens_in[k].reshape(raw, chunk)

    def mine(way, k):
        return jnp.dot(slots[way], here(k), preferred_element_type=jnp.float32)

    def begin(way, k):
        lines[k, way] = mine(way, k).astype(jnp.bfloat16)
        stream_copy(way, k).start()

    def relay(way, k):
        stream_copy(way, k).wait_recv()
        lines[k, way] = (lines[k, way].astype(jnp.float32) + mine(way, k)).astype(jnp.bfloat16)
        stream_copy(way, k).start()

    def lead(position, k):
        for way in range(2):
            @pl.when(chip == (position, last - position)[way])
            def _():
                own_read(feats[k // per_layer], k).wait()
                near_copy(feats[k // per_layer], k, 1 - core).wait_recv()
                if position == 0:
                    begin(way, k)
                else:
                    relay(way, k)

    def pair_copy(k):
        return pltpu.make_async_remote_copy(
            src_ref=joined.at[0, k],
            dst_ref=joined.at[1, k],
            send_sem=pair_send.at[k],
            recv_sem=pair_recv.at[k],
            device_id={"grp": sibling},
            device_id_type=mesh_id,
        )

    def follow(k):
        for way in range(2):
            @pl.when(chip == (last, 0)[way])
            def _():
                stream_copy(way, k).wait_recv()

            @pl.when((chip < last) & (chip >= chips // 2) if way == 0 else (chip > 0) & (chip < chips // 2))
            def _():
                relay(way, k)

        seen = jnp.concatenate([lines[k, 0], here(k), lines[k, 1]], axis=0)
        joined[0, k] = jnp.dot(place[...], seen, preferred_element_type=jnp.float32).astype(
            jnp.bfloat16
        )
        pair_copy(k).start()

    def part_copy(d, h):
        target = lax.rem(own + d, owners)
        return pltpu.make_async_remote_copy(
            src_ref=sums.at[h, pl.ds(pl.multiple_of(target * room, 8), room), :],
            dst_ref=parts.at[d - 1, h],
            send_sem=part_send.at[d - 1, h],
            recv_sem=part_recv.at[d - 1, h],
            device_id={"tp": target},
            device_id_type=mesh_id,
        )

    def multiply(k, first, final):
        for side in range(2):
            weight_copy(k, side).wait()
        pair_copy(k).wait_recv()

        def columns_of(h):
            cols = pl.ds(pl.multiple_of(h * piece, piece), piece)

            def product(side):
                return jnp.dot(
                    joined[side, k], weights[k, side, :, cols], preferred_element_type=jnp.float32
                )

            value = product(0) + product(1)
            if first:
                sums[h] = value
            else:
                sums[h] += value

        if final:
            for h in range(pieces):
                columns_of(h)
                for d in range(1, owners):
                    part_copy(d, h).start()
        else:
            pl.loop(0, pieces)(columns_of)

    leads = [2 * (last - 2 * position) for position in range(chips // 2)]
    for position, a in enumerate(leads):
        for k in range(min(a, chunks)):
            lead(position, k)
    for k in range(chunks):
        for position, a in enumerate(leads):
            if k + a < chunks:
                lead(position, k + a)
        follow(k)
        if k > 0:
            multiply(k - 1, k == 1, False)
    multiply(chunks - 1, False, True)

    def reduce(h, square):
        whole = sums[h, pl.ds(pl.multiple_of(own * room, 8), room), :]
        for d in range(1, owners):
            part_copy(d, h).wait_recv()
            whole = whole + parts[d - 1, h]
        parts[owners - 1, h] = whole
        return square + jnp.sum(whole * whole, axis=1, keepdims=True)

    square = lax.fori_loop(0, pieces, reduce, jnp.zeros((room, 1), jnp.float32))
    diagonal = lax.broadcasted_iota(jnp.int32, (room, 128), 0) == lax.broadcasted_iota(
        jnp.int32, (room, 128), 1
    )
    lanes = jnp.sum(jnp.where(diagonal, square, 0.0), axis=0, keepdims=True)
    squares[0] = jnp.broadcast_to(lanes, (8, 128))

    def square_copy(d):
        return pltpu.make_async_remote_copy(
            src_ref=squares.at[0],
            dst_ref=squares.at[d],
            send_sem=sq_send.at[d - 1],
            recv_sem=sq_recv.at[d - 1],
            device_id={"grp": lax.rem(me + d, groups)},
            device_id_type=mesh_id,
        )

    for d in range(1, groups):
        square_copy(d).start()
    for d in range(1, groups):
        square_copy(d).wait_recv()
    lanes = squares[0]
    for d in range(1, groups):
        lanes = lanes + squares[d]
    square = jnp.sum(jnp.where(diagonal, lanes[0:1], 0.0), axis=1, keepdims=True)
    inverse = lax.rsqrt(square / width + EPSILON)
    for h in range(pieces):
        cols = slice(h * piece, (h + 1) * piece)
        normed = (parts[owners - 1, h] * inverse * gain_ref[:, cols]).astype(jnp.bfloat16)
        out_ref[:, cols] = jnp.dot(
            spread[...], normed, preferred_element_type=jnp.float32
        ).astype(jnp.bfloat16)

    for k in range(chunks):
        for way in range(2):
            @pl.when(passes_on(way))
            def _():
                stream_copy(way, k).wait_send()

        pair_copy(k).wait_send()
    for k in range(chunks):
        near_copy(feats[k // per_layer], k, core).wait_send()
    for d in range(1, owners):
        for h in range(pieces):
            part_copy(d, h).wait_send()
    for d in range(1, groups):
        square_copy(d).wait_send()


def fast_call(groups, owners, hop, room, collective_id, *args):
    tokens, depth = args[0].shape
    columns = args[3].shape[1]
    rows = args[7].shape[0]
    slab = rows * POS // owners
    half = depth // 2
    chunk = min(CHUNK, half)
    chunks = LAYERS * half // chunk
    piece = min(PIECE, columns)
    pieces = columns // piece
    wide = 2 * hop + 2 * tokens

    vmem = pl.BlockSpec(memory_space=pltpu.VMEM)
    hbm = pl.BlockSpec(memory_space=pl.ANY)
    smem = pl.BlockSpec(memory_space=pltpu.SMEM)
    dma = pltpu.SemaphoreType.DMA
    return pl.pallas_call(
        functools.partial(fast_kernel, groups, owners, hop, room),
        out_shape=jax.ShapeDtypeStruct((slab, columns), jnp.bfloat16),
        in_specs=[hbm] * 6 + [vmem] + [smem] * 2,
        out_specs=vmem,
        scratch_shapes=[
            pltpu.VMEM((chunks, 2, hop, chunk), jnp.bfloat16),
            pltpu.VMEM((chunks, 2, tokens, chunk), jnp.bfloat16),
            pltpu.VMEM((chunks, 2, chunk, columns), jnp.bfloat16),
            pltpu.VMEM((2, chunks, owners * room, chunk), jnp.bfloat16),
            pltpu.VMEM((pieces, owners * room, piece), jnp.float32),
            pltpu.VMEM((owners, pieces, room, piece), jnp.float32),
            pltpu.VMEM((groups, 8, 128), jnp.float32),
            pltpu.VMEM((2, hop, 2 * tokens), jnp.bfloat16),
            pltpu.VMEM((owners * room, wide), jnp.bfloat16),
            pltpu.VMEM((slab, room), jnp.bfloat16),
            pltpu.SMEM((rows,), jnp.int32),
            dma((chunks,)),
            dma((chunks,)),
            dma((chunks,)),
            dma((chunks, 2)),
            dma((2, chunks)),
            dma((2, chunks)),
            dma((chunks,)),
            dma((chunks,)),
            dma((owners - 1, pieces)),
            dma((owners - 1, pieces)),
            dma((groups - 1,)),
            dma((groups - 1,)),
        ],
        compiler_params=pltpu.CompilerParams(
            collective_id=collective_id, has_side_effects=True, vmem_limit_bytes=67043328
        ),
    )(*args[:6], args[6][None, :], *args[7:])


def per_device(groups, owners, *args):
    accepted, assignment = args[7:]
    rows = accepted.shape[0]
    slab = rows * POS // owners
    sizes = [(groups * CAPACITY // 2, slab // 2)]

    count = accepted + 1
    row = jnp.arange(rows, dtype=jnp.int32)
    chip = 2 * ROWS_G
    passed = jnp.maximum(
        jnp.sum(jnp.where(row >= chip, count, 0)), jnp.sum(jnp.where(row < rows - chip, count, 0))
    )
    taken = jnp.where(assignment[:, None] == row[None, :], count[None, :], 0)
    owned = jnp.max(jnp.sum(taken.reshape(owners, -1), axis=1))
    too_small = sum(((passed > hop) | (owned > room)).astype(jnp.int32) for hop, room in sizes)
    calls = [
        functools.partial(fast_call, groups, owners, hop, room, 1 + i)
        for i, (hop, room) in enumerate(sizes)
    ]
    return lax.switch(too_small, calls + [functools.partial(full_call, groups, owners)], *args)


def solution(mesh):
    in_specs = (
        P("grp", "tp"),
        P("grp", "tp"),
        P("grp", "tp"),
        P("tp", "grp"),
        P("tp", "grp"),
        P("tp", "grp"),
        P("grp"),
        P(),
        P(),
    )
    return jax.shard_map(
        functools.partial(per_device, mesh.shape["grp"], mesh.shape["tp"]),
        mesh=mesh,
        in_specs=in_specs,
        out_specs=P("tp", "grp"),
        check_vma=False,
    )
```

```python
import functools

import jax
import jax.numpy as jnp
from jax import lax
from jax.experimental import pallas as pl
from jax.experimental.pallas import tpu as pltpu
from jax.sharding import PartitionSpec as P

ROWS_G = 8
POS = 6
CAPACITY = 4 * ROWS_G
BATCHES = 2
SLOTS = CAPACITY // BATCHES
LAYERS = 3
STEPS = BATCHES * LAYERS
AHEAD = 2
TILE = 256
PIECES = 1
EPSILON = 1e-05


def kernel(
    groups, owners,
    low_ref, mid_ref, high_ref, w_low, w_mid, w_high, gain_ref, accepted_ref, assignment_ref,
    out_ref,
    feats, weights, blocks, sums, parts, squares, rows_out, pick,
    f_sem, w_sem, send_sem, recv_sem, part_send, part_recv, sq_send, sq_recv, row_send, row_recv,
):
    me = lax.axis_index("grp")
    own = lax.axis_index("tp")
    chip, core = me // 2, me % 2
    chips = groups // 2
    sibling = chip * 2 + 1 - core
    columns = sums.shape[2]
    share = rows_out.shape[2]
    width = groups * columns
    tiles = columns // TILE
    tokens = feats.shape[1]
    slab = out_ref.shape[0]
    pair_slots = 2 * CAPACITY // ROWS_G

    reads = [
        pltpu.make_async_copy(f, feats.at[i], f_sem.at[i])
        for i, f in enumerate((low_ref, mid_ref, high_ref))
    ]
    for read in reads:
        read.start()
    loads = [
        pltpu.make_async_copy(w, weights.at[i], w_sem.at[i])
        for i, w in enumerate((w_low, w_mid, w_high))
    ]

    barrier = pltpu.get_barrier_semaphore()
    for d in range(1, groups):
        pl.semaphore_signal(
            barrier, inc=1, device_id={"grp": lax.rem(me + d, groups)},
            device_id_type=pl.DeviceIdType.MESH,
        )
    for d in range(1, owners):
        pl.semaphore_signal(
            barrier, inc=1, device_id={"tp": lax.rem(own + d, owners)},
            device_id_type=pl.DeviceIdType.MESH,
        )

    def rows_of(group):
        return pl.ds(pl.multiple_of(group * SLOTS, SLOTS), SLOTS)

    slot = lax.broadcasted_iota(jnp.int32, (CAPACITY, tokens), 0)
    token = lax.broadcasted_iota(jnp.int32, (CAPACITY, tokens), 1)
    packing = jnp.zeros((CAPACITY, tokens), jnp.float32)
    for k in range(ROWS_G):
        count = accepted_ref[me * ROWS_G + k] + 1
        start = (k // 2) * pair_slots
        if k % 2 == 1:
            start = start + accepted_ref[me * ROWS_G + k - 1] + 1
        position = token - k * POS
        hit = (position >= 0) & (position < count) & (slot == start + position)
        packing = jnp.where(hit, 1.0, packing)
    packing = packing.astype(jnp.bfloat16)

    def pack(layer):
        reads[layer].wait()
        packed = jnp.dot(packing, feats[layer], preferred_element_type=jnp.float32)
        for b in range(BATCHES):
            blocks[b * LAYERS + layer, rows_of(me), :] = packed[
                b * SLOTS : (b + 1) * SLOTS
            ].astype(jnp.bfloat16)

    pack(0)
    pl.semaphore_wait(barrier, groups + owners - 2)

    def block_copy(way, step, group):
        target = (chip * 2 + 2 + core, chip * 2 - 2 + core, sibling)[way]
        return pltpu.make_async_remote_copy(
            src_ref=blocks.at[step, rows_of(group), :],
            dst_ref=blocks.at[step, rows_of(group), :],
            send_sem=send_sem.at[way, step, group // 2],
            recv_sem=recv_sem.at[step, group],
            device_id={"grp": target},
            device_id_type=pl.DeviceIdType.MESH,
        )

    def send_own(step):
        @pl.when(chip < chips - 1)
        def _():
            block_copy(0, step, me).start()

        @pl.when(chip > 0)
        def _():
            block_copy(1, step, me).start()

        block_copy(2, step, me).start()

    def relay(step, d):
        @pl.when(chip - d >= 0)
        def _():
            group = me - 2 * d
            block_copy(0, step, group).wait_recv()

            @pl.when(chip < chips - 1)
            def _():
                block_copy(0, step, group).start()

            block_copy(2, step, group).start()

        @pl.when(chip + d <= chips - 1)
        def _():
            group = me + 2 * d
            block_copy(1, step, group).wait_recv()

            @pl.when(chip > 0)
            def _():
                block_copy(1, step, group).start()

            block_copy(2, step, group).start()

    def relays(step, first, last):
        @pl.loop(first, last)
        def _(d):
            relay(step, d)

    def arrive(step):
        for q in range(chips):
            block_copy(2, step, q * 2 + 1 - core).wait_recv()

    def multiply(step):
        b, layer = step // LAYERS, step % LAYERS

        @pl.loop(0, tiles)
        def _(j):
            cols = pl.ds(pl.multiple_of(j * TILE, TILE), TILE)
            product = jnp.dot(
                blocks[step], weights[layer, :, cols], preferred_element_type=jnp.float32
            )
            if layer == 0:
                sums[b, :, cols] = product
            else:
                sums[b, :, cols] += product
            if layer == LAYERS - 1:
                @pl.when(j % piece_tiles == piece_tiles - 1)
                def _():
                    for d in range(1, owners):
                        part_copy(b, d, j // piece_tiles).start()

            if step + 1 < STEPS:
                relays(
                    step + 1,
                    1 + (chips - 1) * j // tiles,
                    1 + (chips - 1) * (j + 1) // tiles,
                )
            if b > 0 and layer == 1:
                @pl.when(j == tiles // 2)
                def _():
                    reduce(b - 1)

    def share_of(owner):
        return pl.ds(pl.multiple_of(owner * share, share), share)

    piece = columns // PIECES
    piece_tiles = tiles // PIECES

    def part_copy(b, d, h):
        cols = pl.ds(pl.multiple_of(h * piece, piece), piece)
        target = lax.rem(own + d, owners)
        return pltpu.make_async_remote_copy(
            src_ref=sums.at[b, share_of(target), cols],
            dst_ref=parts.at[b, d - 1, :, cols],
            send_sem=part_send.at[b, d - 1, h],
            recv_sem=part_recv.at[b, d - 1, h],
            device_id={"tp": target},
            device_id_type=pl.DeviceIdType.MESH,
        )

    def square_copy(b, d):
        return pltpu.make_async_remote_copy(
            src_ref=squares.at[b, 0],
            dst_ref=squares.at[b, d],
            send_sem=sq_send.at[b, d - 1],
            recv_sem=sq_recv.at[b, d - 1],
            device_id={"grp": lax.rem(me + d, groups)},
            device_id_type=pl.DeviceIdType.MESH,
        )

    def row_copy(b, d):
        return pltpu.make_async_remote_copy(
            src_ref=rows_out.at[b, own],
            dst_ref=rows_out.at[b, own],
            send_sem=row_send.at[b, d - 1],
            recv_sem=row_recv.at[b, d - 1],
            device_id={"tp": lax.rem(own + d, owners)},
            device_id_type=pl.DeviceIdType.MESH,
        )

    diagonal = lax.broadcasted_iota(jnp.int32, (share, 128), 0) == lax.broadcasted_iota(
        jnp.int32, (share, 128), 1
    )

    def reduce(b):
        def body(h, square):
            cols = pl.ds(pl.multiple_of(h * piece, piece), piece)
            total = sums[b, share_of(own), cols]
            for d in range(1, owners):
                part_copy(b, d, h).wait_recv()
                total = total + parts[b, d - 1, :, cols]
            parts[b, owners - 1, :, cols] = total
            return square + jnp.sum(total * total, axis=1, keepdims=True)

        square = lax.fori_loop(0, PIECES, body, jnp.zeros((share, 1), jnp.float32))
        lanes = jnp.sum(jnp.where(diagonal, square, 0.0), axis=0, keepdims=True)
        squares[b, 0] = jnp.broadcast_to(lanes, (8, 128))
        for d in range(1, groups):
            square_copy(b, d).start()

    def finish(b):
        for d in range(1, groups):
            square_copy(b, d).wait_recv()
        lanes = squares[b, 0]
        for d in range(1, groups):
            lanes = lanes + squares[b, d]
        square = jnp.sum(jnp.where(diagonal, lanes[0:1], 0.0), axis=1, keepdims=True)
        inverse = lax.rsqrt(square / width + EPSILON)
        rows_out[b, own] = (parts[b, owners - 1] * inverse * gain_ref[...]).astype(jnp.bfloat16)
        for d in range(1, owners):
            row_copy(b, d).start()

    send_own(0)
    pack(1)
    send_own(1)
    for load in loads:
        load.start()
    pack(2)

    column = lax.broadcasted_iota(jnp.int32, pick.shape, 1)
    batch_rows = groups * SLOTS
    batch_bits, slot_bits = batch_rows.bit_length() - 1, SLOTS.bit_length() - 1
    group_of = lax.shift_right_logical(column & (batch_rows - 1), slot_bits)
    slot_of = lax.shift_right_logical(column, batch_bits) * SLOTS + (column & (SLOTS - 1))
    place = group_of * CAPACITY + slot_of
    line = lax.broadcasted_iota(jnp.int32, pick.shape, 0)
    picking = jnp.zeros(pick.shape, jnp.float32)
    for k in range(slab // POS):
        source = assignment_ref[own * (slab // POS) + k]
        count = accepted_ref[source] + 1
        local = source & (ROWS_G - 1)
        odd = local & 1
        before = (accepted_ref[jnp.maximum(source - 1, 0)] + 1) * odd
        start = (source - local) // ROWS_G * CAPACITY + (local - odd) // 2 * pair_slots + before
        position = line - k * POS
        hit = (position >= 0) & (position < count) & (place == start + position)
        picking = jnp.where(hit, 1.0, picking)
    pick[...] = picking.astype(jnp.bfloat16)

    relays(0, 1, chips)
    arrive(0)
    for step in range(STEPS):
        if step + AHEAD < STEPS:
            send_own(step + AHEAD)
        if step < LAYERS:
            loads[step].wait()
        multiply(step)
        if step + 1 < STEPS:
            arrive(step + 1)
        if step >= LAYERS and step % LAYERS == 2:
            finish(step // LAYERS - 1)
    reduce(BATCHES - 1)
    finish(BATCHES - 1)
    for b in range(BATCHES):
        for d in range(1, owners):
            row_copy(b, d).wait_recv()

    everything = rows_out[...].reshape(BATCHES * owners * share, columns)
    out_ref[...] = jnp.dot(
        pick[...], everything, preferred_element_type=jnp.float32
    ).astype(jnp.bfloat16)

    for step in range(STEPS):
        for q in range(chips):
            group = q * 2 + core

            @pl.when((chip < chips - 1) & (q <= chip))
            def _():
                block_copy(0, step, group).wait_send()

            @pl.when((chip > 0) & (q >= chip))
            def _():
                block_copy(1, step, group).wait_send()

            block_copy(2, step, group).wait_send()
    for b in range(BATCHES):
        for d in range(1, owners):
            for h in range(PIECES):
                part_copy(b, d, h).wait_send()
            row_copy(b, d).wait_send()
        for d in range(1, groups):
            square_copy(b, d).wait_send()


def full_call(
    groups, owners,
    low_feats, mid_feats, high_feats, w_low, w_mid, w_high, norm_gain, accepted, assignment,
):
    tokens, depth = low_feats.shape
    columns = w_low.shape[1]
    rows = accepted.shape[0]
    batch_rows = groups * SLOTS
    share = batch_rows // owners
    slab = rows * POS // owners

    vmem = pl.BlockSpec(memory_space=pltpu.VMEM)
    hbm = pl.BlockSpec(memory_space=pl.ANY)
    smem = pl.BlockSpec(memory_space=pltpu.SMEM)
    dma = pltpu.SemaphoreType.DMA
    return pl.pallas_call(
        functools.partial(kernel, groups, owners),
        out_shape=jax.ShapeDtypeStruct((slab, columns), jnp.bfloat16),
        in_specs=[hbm] * 6 + [vmem] + [smem] * 2,
        out_specs=vmem,
        scratch_shapes=[
            pltpu.VMEM((LAYERS, tokens, depth), jnp.bfloat16),
            pltpu.VMEM((LAYERS, depth, columns), jnp.bfloat16),
            pltpu.VMEM((STEPS, batch_rows, depth), jnp.bfloat16),
            pltpu.VMEM((BATCHES, batch_rows, columns), jnp.float32),
            pltpu.VMEM((BATCHES, owners, share, columns), jnp.float32),
            pltpu.VMEM((BATCHES, groups, 8, 128), jnp.float32),
            pltpu.VMEM((BATCHES, owners, share, columns), jnp.bfloat16),
            pltpu.VMEM((slab, BATCHES * batch_rows), jnp.bfloat16),
            dma((LAYERS,)),
            dma((LAYERS,)),
            dma((3, STEPS, groups // 2)),
            dma((STEPS, groups)),
            dma((BATCHES, owners - 1, PIECES)),
            dma((BATCHES, owners - 1, PIECES)),
            dma((BATCHES, groups - 1)),
            dma((BATCHES, groups - 1)),
            dma((BATCHES, owners - 1)),
            dma((BATCHES, owners - 1)),
        ],
        compiler_params=pltpu.CompilerParams(
            collective_id=0, has_side_effects=True, vmem_limit_bytes=67043328
        ),
    )(low_feats, mid_feats, high_feats, w_low, w_mid, w_high, norm_gain[None, :], accepted, assignment)


CHUNK = 512
PIECE = 512


def fast_kernel(
    groups, owners, hop, room,
    low_ref, mid_ref, high_ref, w_low, w_mid, w_high, gain_ref, accepted_ref, assignment_ref,
    out_ref,
    lines, tokens_in, weights, joined, sums, parts, squares, slots, place, spread, before,
    raw_sem, near_sem, near_send, w_sem, hop_send, hop_recv, pair_send, pair_recv,
    part_send, part_recv, sq_send, sq_recv,
):
    me = lax.axis_index("grp")
    own = lax.axis_index("tp")
    chip, core = me // 2, me % 2
    chips = groups // 2
    last = chips - 1
    sibling = chip * 2 + 1 - core
    feats = (low_ref, mid_ref, high_ref)
    tokens, depth = low_ref.shape
    pieces, _, piece = sums.shape
    columns = pieces * piece
    half = depth // 2
    chunk = joined.shape[3]
    per_layer = half // chunk
    chunks = LAYERS * per_layer
    rows = accepted_ref.shape[0]
    slab = out_ref.shape[0]
    row_slots = slab // POS
    chip_rows = 2 * ROWS_G
    raw = 2 * tokens
    width = groups * columns
    mesh_id = pl.DeviceIdType.MESH

    barrier = pltpu.get_barrier_semaphore()
    for d in range(1, groups):
        pl.semaphore_signal(
            barrier, inc=1, device_id={"grp": lax.rem(me + d, groups)}, device_id_type=mesh_id
        )
    for d in range(1, owners):
        pl.semaphore_signal(
            barrier, inc=1, device_id={"tp": lax.rem(own + d, owners)}, device_id_type=mesh_id
        )

    def feature_cols(which, part):
        return pl.ds(pl.multiple_of(which * half + part * chunk, chunk), chunk)

    def own_read(f, k):
        return pltpu.make_async_copy(
            f.at[:, feature_cols(core, k % per_layer)], tokens_in.at[k, core], raw_sem.at[k]
        )

    def near_copy(f, k, side):
        return pltpu.make_async_remote_copy(
            src_ref=f.at[:, feature_cols(1 - core, k % per_layer)],
            dst_ref=tokens_in.at[k, side],
            send_sem=near_send.at[k],
            recv_sem=near_sem.at[k],
            device_id={"grp": sibling},
            device_id_type=mesh_id,
        )

    for k in range(chunks):
        own_read(feats[k // per_layer], k).start()

    def weight_copy(k, side):
        which = core + side - 2 * core * side
        at = pl.ds(pl.multiple_of(which * half + k % per_layer * chunk, chunk), chunk)
        return pltpu.make_async_copy(
            (w_low, w_mid, w_high)[k // per_layer].at[at, :], weights.at[k, side], w_sem.at[k, side]
        )

    for k in range(chunks):
        for side in range(2):
            weight_copy(k, side).start()

    def count_row(r, total):
        before[r] = total
        return total + accepted_ref[r] + 1

    total = lax.fori_loop(0, rows, count_row, jnp.int32(0))

    token = lax.broadcasted_iota(jnp.int32, (1, raw), 1)
    slot = jnp.full((1, raw), -1, jnp.int32)
    for k in range(chip_rows):
        r = chip * chip_rows + k
        position = token - k * POS
        hit = (position >= 0) & (position <= accepted_ref[r])
        slot = jnp.where(hit, before[r] + position, slot)
    line = lax.broadcasted_iota(jnp.int32, (hop, raw), 0)
    slots[0] = jnp.where(line == slot, 1.0, 0.0).astype(jnp.bfloat16)
    from_end = jnp.where(slot >= 0, slot + (hop - total), -1)
    slots[1] = jnp.where(line == from_end, 1.0, 0.0).astype(jnp.bfloat16)

    lane = lax.broadcasted_iota(jnp.int32, (1, 2 * hop + raw), 1)

    def place_row(j, carry):
        dest, used = carry
        used = jnp.where(j % row_slots == 0, 0, used)
        r = assignment_ref[j]
        first = before[r]
        local = r - chip * chip_rows
        start = jnp.where(
            local < 0,
            first,
            jnp.where(local < chip_rows, hop + local * POS, hop + raw + hop - total + first),
        )
        position = lane - start
        hit = (position >= 0) & (position <= accepted_ref[r])
        dest = jnp.where(hit, j // row_slots * room + used + position, dest)
        return dest, used + accepted_ref[r] + 1

    dest, _ = lax.fori_loop(
        0, rows, place_row, (jnp.full(lane.shape, -1, jnp.int32), jnp.int32(0))
    )
    line = lax.broadcasted_iota(jnp.int32, place.shape, 0)
    place[...] = jnp.where(line == dest, 1.0, 0.0).astype(jnp.bfloat16)

    line = lax.broadcasted_iota(jnp.int32, spread.shape, 0)
    column = lax.broadcasted_iota(jnp.int32, spread.shape, 1)
    spreading = jnp.zeros(spread.shape, jnp.float32)
    used = jnp.int32(0)
    for k in range(row_slots):
        more = accepted_ref[assignment_ref[own * row_slots + k]]
        position = line - k * POS
        hit = (position >= 0) & (position <= more) & (column == used + position)
        spreading = jnp.where(hit, 1.0, spreading)
        used = used + more + 1
    spread[...] = spreading.astype(jnp.bfloat16)

    pl.semaphore_wait(barrier, groups + owners - 2)
    for k in range(chunks):
        near_copy(feats[k // per_layer], k, core).start()

    def stream_copy(way, k):
        return pltpu.make_async_remote_copy(
            src_ref=lines.at[k, way],
            dst_ref=lines.at[k, way],
            send_sem=hop_send.at[way, k],
            recv_sem=hop_recv.at[way, k],
            device_id={"grp": (me + 2, me - 2)[way]},
            device_id_type=mesh_id,
        )

    def passes_on(way):
        return (chip < last, chip > 0)[way]

    def here(k):
        return tokens_in[k].reshape(raw, chunk)

    def mine(way, k):
        return jnp.dot(slots[way], here(k), preferred_element_type=jnp.float32)

    def begin(way, k):
        lines[k, way] = mine(way, k).astype(jnp.bfloat16)
        stream_copy(way, k).start()

    def relay(way, k):
        stream_copy(way, k).wait_recv()
        lines[k, way] = (lines[k, way].astype(jnp.float32) + mine(way, k)).astype(jnp.bfloat16)
        stream_copy(way, k).start()

    def lead(position, k):
        for way in range(2):
            @pl.when(chip == (position, last - position)[way])
            def _():
                own_read(feats[k // per_layer], k).wait()
                near_copy(feats[k // per_layer], k, 1 - core).wait_recv()
                if position == 0:
                    begin(way, k)
                else:
                    relay(way, k)

    def pair_copy(k):
        return pltpu.make_async_remote_copy(
            src_ref=joined.at[0, k],
            dst_ref=joined.at[1, k],
            send_sem=pair_send.at[k],
            recv_sem=pair_recv.at[k],
            device_id={"grp": sibling},
            device_id_type=mesh_id,
        )

    def follow(k):
        for way in range(2):
            @pl.when(chip == (last, 0)[way])
            def _():
                stream_copy(way, k).wait_recv()

            @pl.when((chip < last) & (chip >= chips // 2) if way == 0 else (chip > 0) & (chip < chips // 2))
            def _():
                relay(way, k)

        seen = jnp.concatenate([lines[k, 0], here(k), lines[k, 1]], axis=0)
        joined[0, k] = jnp.dot(place[...], seen, preferred_element_type=jnp.float32).astype(
            jnp.bfloat16
        )
        pair_copy(k).start()

    def part_copy(d, h):
        target = lax.rem(own + d, owners)
        return pltpu.make_async_remote_copy(
            src_ref=sums.at[h, pl.ds(pl.multiple_of(target * room, 8), room), :],
            dst_ref=parts.at[d - 1, h],
            send_sem=part_send.at[d - 1, h],
            recv_sem=part_recv.at[d - 1, h],
            device_id={"tp": target},
            device_id_type=mesh_id,
        )

    def multiply(k, first, final):
        for side in range(2):
            weight_copy(k, side).wait()
        pair_copy(k).wait_recv()

        def columns_of(h):
            cols = pl.ds(pl.multiple_of(h * piece, piece), piece)

            def product(side):
                return jnp.dot(
                    joined[side, k], weights[k, side, :, cols], preferred_element_type=jnp.float32
                )

            value = product(0) + product(1)
            if first:
                sums[h] = value
            else:
                sums[h] += value

        if final:
            for h in range(pieces):
                columns_of(h)
                for d in range(1, owners):
                    part_copy(d, h).start()
        else:
            pl.loop(0, pieces)(columns_of)

    leads = [2 * (last - 2 * position) for position in range(chips // 2)]
    for position, a in enumerate(leads):
        for k in range(min(a, chunks)):
            lead(position, k)
    for k in range(chunks):
        for position, a in enumerate(leads):
            if k + a < chunks:
                lead(position, k + a)
        follow(k)
        if k > 0:
            multiply(k - 1, k == 1, False)
    multiply(chunks - 1, False, True)

    def reduce(h, square):
        whole = sums[h, pl.ds(pl.multiple_of(own * room, 8), room), :]
        for d in range(1, owners):
            part_copy(d, h).wait_recv()
            whole = whole + parts[d - 1, h]
        parts[owners - 1, h] = whole
        return square + jnp.sum(whole * whole, axis=1, keepdims=True)

    square = lax.fori_loop(0, pieces, reduce, jnp.zeros((room, 1), jnp.float32))
    diagonal = lax.broadcasted_iota(jnp.int32, (room, 128), 0) == lax.broadcasted_iota(
        jnp.int32, (room, 128), 1
    )
    lanes = jnp.sum(jnp.where(diagonal, square, 0.0), axis=0, keepdims=True)
    squares[0] = jnp.broadcast_to(lanes, (8, 128))

    def square_copy(d):
        return pltpu.make_async_remote_copy(
            src_ref=squares.at[0],
            dst_ref=squares.at[d],
            send_sem=sq_send.at[d - 1],
            recv_sem=sq_recv.at[d - 1],
            device_id={"grp": lax.rem(me + d, groups)},
            device_id_type=mesh_id,
        )

    for d in range(1, groups):
        square_copy(d).start()
    for d in range(1, groups):
        square_copy(d).wait_recv()
    lanes = squares[0]
    for d in range(1, groups):
        lanes = lanes + squares[d]
    square = jnp.sum(jnp.where(diagonal, lanes[0:1], 0.0), axis=1, keepdims=True)
    inverse = lax.rsqrt(square / width + EPSILON)
    for h in range(pieces):
        cols = slice(h * piece, (h + 1) * piece)
        normed = (parts[owners - 1, h] * inverse * gain_ref[:, cols]).astype(jnp.bfloat16)
        out_ref[:, cols] = jnp.dot(
            spread[...], normed, preferred_element_type=jnp.float32
        ).astype(jnp.bfloat16)

    for k in range(chunks):
        for way in range(2):
            @pl.when(passes_on(way))
            def _():
                stream_copy(way, k).wait_send()

        pair_copy(k).wait_send()
    for k in range(chunks):
        near_copy(feats[k // per_layer], k, core).wait_send()
    for d in range(1, owners):
        for h in range(pieces):
            part_copy(d, h).wait_send()
    for d in range(1, groups):
        square_copy(d).wait_send()


def fast_call(groups, owners, hop, room, collective_id, *args):
    tokens, depth = args[0].shape
    columns = args[3].shape[1]
    rows = args[7].shape[0]
    slab = rows * POS // owners
    half = depth // 2
    chunk = min(CHUNK, half)
    chunks = LAYERS * half // chunk
    piece = min(PIECE, columns)
    pieces = columns // piece
    wide = 2 * hop + 2 * tokens

    vmem = pl.BlockSpec(memory_space=pltpu.VMEM)
    hbm = pl.BlockSpec(memory_space=pl.ANY)
    smem = pl.BlockSpec(memory_space=pltpu.SMEM)
    dma = pltpu.SemaphoreType.DMA
    return pl.pallas_call(
        functools.partial(fast_kernel, groups, owners, hop, room),
        out_shape=jax.ShapeDtypeStruct((slab, columns), jnp.bfloat16),
        in_specs=[hbm] * 6 + [vmem] + [smem] * 2,
        out_specs=vmem,
        scratch_shapes=[
            pltpu.VMEM((chunks, 2, hop, chunk), jnp.bfloat16),
            pltpu.VMEM((chunks, 2, tokens, chunk), jnp.bfloat16),
            pltpu.VMEM((chunks, 2, chunk, columns), jnp.bfloat16),
            pltpu.VMEM((2, chunks, owners * room, chunk), jnp.bfloat16),
            pltpu.VMEM((pieces, owners * room, piece), jnp.float32),
            pltpu.VMEM((owners, pieces, room, piece), jnp.float32),
            pltpu.VMEM((groups, 8, 128), jnp.float32),
            pltpu.VMEM((2, hop, 2 * tokens), jnp.bfloat16),
            pltpu.VMEM((owners * room, wide), jnp.bfloat16),
            pltpu.VMEM((slab, room), jnp.bfloat16),
            pltpu.SMEM((rows,), jnp.int32),
            dma((chunks,)),
            dma((chunks,)),
            dma((chunks,)),
            dma((chunks, 2)),
            dma((2, chunks)),
            dma((2, chunks)),
            dma((chunks,)),
            dma((chunks,)),
            dma((owners - 1, pieces)),
            dma((owners - 1, pieces)),
            dma((groups - 1,)),
            dma((groups - 1,)),
        ],
        compiler_params=pltpu.CompilerParams(
            collective_id=collective_id, has_side_effects=True, vmem_limit_bytes=67043328
        ),
    )(*args[:6], args[6][None, :], *args[7:])


def choose(sizes, owners, accepted_ref, assignment_ref, which_ref):
    rows = accepted_ref.shape[0]
    chip_rows = 2 * ROWS_G

    def add_row(r, carry):
        low, high = carry
        count = accepted_ref[r] + 1
        return low + jnp.where(r < chip_rows, 0, count), high + jnp.where(r < rows - chip_rows, count, 0)

    low, high = lax.fori_loop(0, rows, add_row, (jnp.int32(0), jnp.int32(0)), unroll=8)
    passed = jnp.maximum(low, high)

    def add_slot(j, carry):
        used, most = carry
        used = jnp.where(j % (rows // owners) == 0, 0, used) + accepted_ref[assignment_ref[j]] + 1
        return used, jnp.maximum(most, used)

    _, owned = lax.fori_loop(0, rows, add_slot, (jnp.int32(0), jnp.int32(0)), unroll=8)
    which = jnp.int32(0)
    for hop, room in sizes:
        which = which + jnp.where((passed > hop) | (owned > room), 1, 0)
    which_ref[0] = which


def per_device(groups, owners, *args):
    accepted, assignment = args[7:]
    rows = accepted.shape[0]
    slab = rows * POS // owners
    sizes = [(groups * CAPACITY * 7 // 16 // 16 * 16, slab * 5 // 12), (groups * CAPACITY // 2, slab // 2)]
    smem = pl.BlockSpec(memory_space=pltpu.SMEM)
    which = pl.pallas_call(
        functools.partial(choose, sizes, owners),
        out_shape=jax.ShapeDtypeStruct((1,), jnp.int32),
        in_specs=[smem] * 2,
        out_specs=smem,
    )(accepted, assignment)
    calls = [
        functools.partial(fast_call, groups, owners, hop, room, 1 + i)
        for i, (hop, room) in enumerate(sizes)
    ]
    return lax.switch(which[0], calls + [functools.partial(full_call, groups, owners)], *args)


def solution(mesh):
    in_specs = (
        P("grp", "tp"),
        P("grp", "tp"),
        P("grp", "tp"),
        P("tp", "grp"),
        P("tp", "grp"),
        P("tp", "grp"),
        P("grp"),
        P(),
        P(),
    )
    return jax.shard_map(
        functools.partial(per_device, mesh.shape["grp"], mesh.shape["tp"]),
        mesh=mesh,
        in_specs=in_specs,
        out_specs=P("tp", "grp"),
        check_vma=False,
    )
```

```python
import functools

import jax
import jax.numpy as jnp
from jax import lax
from jax.experimental import pallas as pl
from jax.experimental.pallas import tpu as pltpu
from jax.sharding import PartitionSpec as P

ROWS_G = 8
POS = 6
CAPACITY = 4 * ROWS_G
BATCHES = 2
SLOTS = CAPACITY // BATCHES
LAYERS = 3
STEPS = BATCHES * LAYERS
AHEAD = 2
TILE = 256
PIECES = 1
EPSILON = 1e-05


def kernel(
    groups, owners,
    low_ref, mid_ref, high_ref, w_low, w_mid, w_high, gain_ref, accepted_ref, assignment_ref,
    out_ref,
    feats, weights, blocks, sums, parts, squares, rows_out, pick,
    f_sem, w_sem, send_sem, recv_sem, part_send, part_recv, sq_send, sq_recv, row_send, row_recv,
):
    me = lax.axis_index("grp")
    own = lax.axis_index("tp")
    chip, core = me // 2, me % 2
    chips = groups // 2
    sibling = chip * 2 + 1 - core
    columns = sums.shape[2]
    share = rows_out.shape[2]
    width = groups * columns
    tiles = columns // TILE
    tokens = feats.shape[1]
    slab = out_ref.shape[0]
    pair_slots = 2 * CAPACITY // ROWS_G

    reads = [
        pltpu.make_async_copy(f, feats.at[i], f_sem.at[i])
        for i, f in enumerate((low_ref, mid_ref, high_ref))
    ]
    for read in reads:
        read.start()
    loads = [
        pltpu.make_async_copy(w, weights.at[i], w_sem.at[i])
        for i, w in enumerate((w_low, w_mid, w_high))
    ]

    barrier = pltpu.get_barrier_semaphore()
    for d in range(1, groups):
        pl.semaphore_signal(
            barrier, inc=1, device_id={"grp": lax.rem(me + d, groups)},
            device_id_type=pl.DeviceIdType.MESH,
        )
    for d in range(1, owners):
        pl.semaphore_signal(
            barrier, inc=1, device_id={"tp": lax.rem(own + d, owners)},
            device_id_type=pl.DeviceIdType.MESH,
        )

    def rows_of(group):
        return pl.ds(pl.multiple_of(group * SLOTS, SLOTS), SLOTS)

    slot = lax.broadcasted_iota(jnp.int32, (CAPACITY, tokens), 0)
    token = lax.broadcasted_iota(jnp.int32, (CAPACITY, tokens), 1)
    packing = jnp.zeros((CAPACITY, tokens), jnp.float32)
    for k in range(ROWS_G):
        count = accepted_ref[me * ROWS_G + k] + 1
        start = (k // 2) * pair_slots
        if k % 2 == 1:
            start = start + accepted_ref[me * ROWS_G + k - 1] + 1
        position = token - k * POS
        hit = (position >= 0) & (position < count) & (slot == start + position)
        packing = jnp.where(hit, 1.0, packing)
    packing = packing.astype(jnp.bfloat16)

    def pack(layer):
        reads[layer].wait()
        packed = jnp.dot(packing, feats[layer], preferred_element_type=jnp.float32)
        for b in range(BATCHES):
            blocks[b * LAYERS + layer, rows_of(me), :] = packed[
                b * SLOTS : (b + 1) * SLOTS
            ].astype(jnp.bfloat16)

    pack(0)
    pl.semaphore_wait(barrier, groups + owners - 2)

    def block_copy(way, step, group):
        target = (chip * 2 + 2 + core, chip * 2 - 2 + core, sibling)[way]
        return pltpu.make_async_remote_copy(
            src_ref=blocks.at[step, rows_of(group), :],
            dst_ref=blocks.at[step, rows_of(group), :],
            send_sem=send_sem.at[way, step, group // 2],
            recv_sem=recv_sem.at[step, group],
            device_id={"grp": target},
            device_id_type=pl.DeviceIdType.MESH,
        )

    def send_own(step):
        @pl.when(chip < chips - 1)
        def _():
            block_copy(0, step, me).start()

        @pl.when(chip > 0)
        def _():
            block_copy(1, step, me).start()

        block_copy(2, step, me).start()

    def relay(step, d):
        @pl.when(chip - d >= 0)
        def _():
            group = me - 2 * d
            block_copy(0, step, group).wait_recv()

            @pl.when(chip < chips - 1)
            def _():
                block_copy(0, step, group).start()

            block_copy(2, step, group).start()

        @pl.when(chip + d <= chips - 1)
        def _():
            group = me + 2 * d
            block_copy(1, step, group).wait_recv()

            @pl.when(chip > 0)
            def _():
                block_copy(1, step, group).start()

            block_copy(2, step, group).start()

    def relays(step, first, last):
        @pl.loop(first, last)
        def _(d):
            relay(step, d)

    def arrive(step):
        for q in range(chips):
            block_copy(2, step, q * 2 + 1 - core).wait_recv()

    def multiply(step):
        b, layer = step // LAYERS, step % LAYERS

        @pl.loop(0, tiles)
        def _(j):
            cols = pl.ds(pl.multiple_of(j * TILE, TILE), TILE)
            product = jnp.dot(
                blocks[step], weights[layer, :, cols], preferred_element_type=jnp.float32
            )
            if layer == 0:
                sums[b, :, cols] = product
            else:
                sums[b, :, cols] += product
            if layer == LAYERS - 1:
                @pl.when(j % piece_tiles == piece_tiles - 1)
                def _():
                    for d in range(1, owners):
                        part_copy(b, d, j // piece_tiles).start()

            if step + 1 < STEPS:
                relays(
                    step + 1,
                    1 + (chips - 1) * j // tiles,
                    1 + (chips - 1) * (j + 1) // tiles,
                )
            if b > 0 and layer == 1:
                @pl.when(j == tiles // 2)
                def _():
                    reduce(b - 1)

    def share_of(owner):
        return pl.ds(pl.multiple_of(owner * share, share), share)

    piece = columns // PIECES
    piece_tiles = tiles // PIECES

    def part_copy(b, d, h):
        cols = pl.ds(pl.multiple_of(h * piece, piece), piece)
        target = lax.rem(own + d, owners)
        return pltpu.make_async_remote_copy(
            src_ref=sums.at[b, share_of(target), cols],
            dst_ref=parts.at[b, d - 1, :, cols],
            send_sem=part_send.at[b, d - 1, h],
            recv_sem=part_recv.at[b, d - 1, h],
            device_id={"tp": target},
            device_id_type=pl.DeviceIdType.MESH,
        )

    def square_copy(b, d):
        return pltpu.make_async_remote_copy(
            src_ref=squares.at[b, 0],
            dst_ref=squares.at[b, d],
            send_sem=sq_send.at[b, d - 1],
            recv_sem=sq_recv.at[b, d - 1],
            device_id={"grp": lax.rem(me + d, groups)},
            device_id_type=pl.DeviceIdType.MESH,
        )

    def row_copy(b, d):
        return pltpu.make_async_remote_copy(
            src_ref=rows_out.at[b, own],
            dst_ref=rows_out.at[b, own],
            send_sem=row_send.at[b, d - 1],
            recv_sem=row_recv.at[b, d - 1],
            device_id={"tp": lax.rem(own + d, owners)},
            device_id_type=pl.DeviceIdType.MESH,
        )

    diagonal = lax.broadcasted_iota(jnp.int32, (share, 128), 0) == lax.broadcasted_iota(
        jnp.int32, (share, 128), 1
    )

    def reduce(b):
        def body(h, square):
            cols = pl.ds(pl.multiple_of(h * piece, piece), piece)
            total = sums[b, share_of(own), cols]
            for d in range(1, owners):
                part_copy(b, d, h).wait_recv()
                total = total + parts[b, d - 1, :, cols]
            parts[b, owners - 1, :, cols] = total
            return square + jnp.sum(total * total, axis=1, keepdims=True)

        square = lax.fori_loop(0, PIECES, body, jnp.zeros((share, 1), jnp.float32))
        lanes = jnp.sum(jnp.where(diagonal, square, 0.0), axis=0, keepdims=True)
        squares[b, 0] = jnp.broadcast_to(lanes, (8, 128))
        for d in range(1, groups):
            square_copy(b, d).start()

    def finish(b):
        for d in range(1, groups):
            square_copy(b, d).wait_recv()
        lanes = squares[b, 0]
        for d in range(1, groups):
            lanes = lanes + squares[b, d]
        square = jnp.sum(jnp.where(diagonal, lanes[0:1], 0.0), axis=1, keepdims=True)
        inverse = lax.rsqrt(square / width + EPSILON)
        rows_out[b, own] = (parts[b, owners - 1] * inverse * gain_ref[...]).astype(jnp.bfloat16)
        for d in range(1, owners):
            row_copy(b, d).start()

    send_own(0)
    pack(1)
    send_own(1)
    for load in loads:
        load.start()
    pack(2)

    column = lax.broadcasted_iota(jnp.int32, pick.shape, 1)
    batch_rows = groups * SLOTS
    batch_bits, slot_bits = batch_rows.bit_length() - 1, SLOTS.bit_length() - 1
    group_of = lax.shift_right_logical(column & (batch_rows - 1), slot_bits)
    slot_of = lax.shift_right_logical(column, batch_bits) * SLOTS + (column & (SLOTS - 1))
    place = group_of * CAPACITY + slot_of
    line = lax.broadcasted_iota(jnp.int32, pick.shape, 0)
    picking = jnp.zeros(pick.shape, jnp.float32)
    for k in range(slab // POS):
        source = assignment_ref[own * (slab // POS) + k]
        count = accepted_ref[source] + 1
        local = source & (ROWS_G - 1)
        odd = local & 1
        before = (accepted_ref[jnp.maximum(source - 1, 0)] + 1) * odd
        start = (source - local) // ROWS_G * CAPACITY + (local - odd) // 2 * pair_slots + before
        position = line - k * POS
        hit = (position >= 0) & (position < count) & (place == start + position)
        picking = jnp.where(hit, 1.0, picking)
    pick[...] = picking.astype(jnp.bfloat16)

    relays(0, 1, chips)
    arrive(0)
    for step in range(STEPS):
        if step + AHEAD < STEPS:
            send_own(step + AHEAD)
        if step < LAYERS:
            loads[step].wait()
        multiply(step)
        if step + 1 < STEPS:
            arrive(step + 1)
        if step >= LAYERS and step % LAYERS == 2:
            finish(step // LAYERS - 1)
    reduce(BATCHES - 1)
    finish(BATCHES - 1)
    for b in range(BATCHES):
        for d in range(1, owners):
            row_copy(b, d).wait_recv()

    everything = rows_out[...].reshape(BATCHES * owners * share, columns)
    out_ref[...] = jnp.dot(
        pick[...], everything, preferred_element_type=jnp.float32
    ).astype(jnp.bfloat16)

    for step in range(STEPS):
        for q in range(chips):
            group = q * 2 + core

            @pl.when((chip < chips - 1) & (q <= chip))
            def _():
                block_copy(0, step, group).wait_send()

            @pl.when((chip > 0) & (q >= chip))
            def _():
                block_copy(1, step, group).wait_send()

            block_copy(2, step, group).wait_send()
    for b in range(BATCHES):
        for d in range(1, owners):
            for h in range(PIECES):
                part_copy(b, d, h).wait_send()
            row_copy(b, d).wait_send()
        for d in range(1, groups):
            square_copy(b, d).wait_send()


def full_call(
    groups, owners,
    low_feats, mid_feats, high_feats, w_low, w_mid, w_high, norm_gain, accepted, assignment,
):
    tokens, depth = low_feats.shape
    columns = w_low.shape[1]
    rows = accepted.shape[0]
    batch_rows = groups * SLOTS
    share = batch_rows // owners
    slab = rows * POS // owners

    vmem = pl.BlockSpec(memory_space=pltpu.VMEM)
    hbm = pl.BlockSpec(memory_space=pl.ANY)
    smem = pl.BlockSpec(memory_space=pltpu.SMEM)
    dma = pltpu.SemaphoreType.DMA
    return pl.pallas_call(
        functools.partial(kernel, groups, owners),
        out_shape=jax.ShapeDtypeStruct((slab, columns), jnp.bfloat16),
        in_specs=[hbm] * 6 + [vmem] + [smem] * 2,
        out_specs=vmem,
        scratch_shapes=[
            pltpu.VMEM((LAYERS, tokens, depth), jnp.bfloat16),
            pltpu.VMEM((LAYERS, depth, columns), jnp.bfloat16),
            pltpu.VMEM((STEPS, batch_rows, depth), jnp.bfloat16),
            pltpu.VMEM((BATCHES, batch_rows, columns), jnp.float32),
            pltpu.VMEM((BATCHES, owners, share, columns), jnp.float32),
            pltpu.VMEM((BATCHES, groups, 8, 128), jnp.float32),
            pltpu.VMEM((BATCHES, owners, share, columns), jnp.bfloat16),
            pltpu.VMEM((slab, BATCHES * batch_rows), jnp.bfloat16),
            dma((LAYERS,)),
            dma((LAYERS,)),
            dma((3, STEPS, groups // 2)),
            dma((STEPS, groups)),
            dma((BATCHES, owners - 1, PIECES)),
            dma((BATCHES, owners - 1, PIECES)),
            dma((BATCHES, groups - 1)),
            dma((BATCHES, groups - 1)),
            dma((BATCHES, owners - 1)),
            dma((BATCHES, owners - 1)),
        ],
        compiler_params=pltpu.CompilerParams(
            collective_id=0, has_side_effects=True, vmem_limit_bytes=67043328
        ),
    )(low_feats, mid_feats, high_feats, w_low, w_mid, w_high, norm_gain[None, :], accepted, assignment)


CHUNK = 512
PIECE = 1024
LEVELS = 32767.0


def fast_kernel(
    groups, owners, hop, room,
    low_ref, mid_ref, high_ref, w_low, w_mid, w_high, gain_ref, accepted_ref, assignment_ref,
    out_ref,
    lines, tokens_in, weights, joined, sums, coded, arrived, scales, scales_in, kept, squares, slots, place, spread, before,
    raw_sem, near_sem, near_send, w_sem, hop_send, hop_recv, pair_send, pair_recv,
    part_send, part_recv, sq_send, sq_recv,
):
    me = lax.axis_index("grp")
    own = lax.axis_index("tp")
    chip, core = me // 2, me % 2
    chips = groups // 2
    last = chips - 1
    sibling = chip * 2 + 1 - core
    feats = (low_ref, mid_ref, high_ref)
    tokens, depth = low_ref.shape
    pieces, _, piece = sums.shape
    columns = pieces * piece
    half = depth // 2
    chunk = joined.shape[3]
    per_layer = half // chunk
    chunks = LAYERS * per_layer
    rows = accepted_ref.shape[0]
    slab = out_ref.shape[0]
    row_slots = slab // POS
    chip_rows = 2 * ROWS_G
    raw = 2 * tokens
    width = groups * columns
    mesh_id = pl.DeviceIdType.MESH

    barrier = pltpu.get_barrier_semaphore()
    for d in range(1, groups):
        pl.semaphore_signal(
            barrier, inc=1, device_id={"grp": lax.rem(me + d, groups)}, device_id_type=mesh_id
        )
    for d in range(1, owners):
        pl.semaphore_signal(
            barrier, inc=1, device_id={"tp": lax.rem(own + d, owners)}, device_id_type=mesh_id
        )

    def feature_cols(which, part):
        return pl.ds(pl.multiple_of(which * half + part * chunk, chunk), chunk)

    def own_read(f, k):
        return pltpu.make_async_copy(
            f.at[:, feature_cols(core, k % per_layer)], tokens_in.at[k, core], raw_sem.at[k]
        )

    def near_copy(f, k, side):
        return pltpu.make_async_remote_copy(
            src_ref=f.at[:, feature_cols(1 - core, k % per_layer)],
            dst_ref=tokens_in.at[k, side],
            send_sem=near_send.at[k],
            recv_sem=near_sem.at[k],
            device_id={"grp": sibling},
            device_id_type=mesh_id,
        )

    for k in range(chunks):
        own_read(feats[k // per_layer], k).start()

    def weight_copy(k, side):
        which = core + side - 2 * core * side
        at = pl.ds(pl.multiple_of(which * half + k % per_layer * chunk, chunk), chunk)
        return pltpu.make_async_copy(
            (w_low, w_mid, w_high)[k // per_layer].at[at, :], weights.at[k, side], w_sem.at[k, side]
        )

    for k in range(chunks):
        for side in range(2):
            weight_copy(k, side).start()

    def count_row(r, total):
        before[r] = total
        return total + accepted_ref[r] + 1

    total = lax.fori_loop(0, rows, count_row, jnp.int32(0))

    token = lax.broadcasted_iota(jnp.int32, (1, raw), 1)
    slot = jnp.full((1, raw), -1, jnp.int32)
    for k in range(chip_rows):
        r = chip * chip_rows + k
        position = token - k * POS
        hit = (position >= 0) & (position <= accepted_ref[r])
        slot = jnp.where(hit, before[r] + position, slot)
    line = lax.broadcasted_iota(jnp.int32, (hop, raw), 0)
    slots[0] = jnp.where(line == slot, 1.0, 0.0).astype(jnp.bfloat16)
    from_end = jnp.where(slot >= 0, slot + (hop - total), -1)
    slots[1] = jnp.where(line == from_end, 1.0, 0.0).astype(jnp.bfloat16)

    lane = lax.broadcasted_iota(jnp.int32, (1, 2 * hop + raw), 1)

    def place_row(j, carry):
        dest, used = carry
        used = jnp.where(j % row_slots == 0, 0, used)
        r = assignment_ref[j]
        first = before[r]
        local = r - chip * chip_rows
        start = jnp.where(
            local < 0,
            first,
            jnp.where(local < chip_rows, hop + local * POS, hop + raw + hop - total + first),
        )
        position = lane - start
        hit = (position >= 0) & (position <= accepted_ref[r])
        dest = jnp.where(hit, j // row_slots * room + used + position, dest)
        return dest, used + accepted_ref[r] + 1

    dest, _ = lax.fori_loop(
        0, rows, place_row, (jnp.full(lane.shape, -1, jnp.int32), jnp.int32(0))
    )
    line = lax.broadcasted_iota(jnp.int32, place.shape, 0)
    place[...] = jnp.where(line == dest, 1.0, 0.0).astype(jnp.bfloat16)

    line = lax.broadcasted_iota(jnp.int32, spread.shape, 0)
    column = lax.broadcasted_iota(jnp.int32, spread.shape, 1)
    spreading = jnp.zeros(spread.shape, jnp.float32)
    used = jnp.int32(0)
    for k in range(row_slots):
        more = accepted_ref[assignment_ref[own * row_slots + k]]
        position = line - k * POS
        hit = (position >= 0) & (position <= more) & (column == used + position)
        spreading = jnp.where(hit, 1.0, spreading)
        used = used + more + 1
    spread[...] = spreading.astype(jnp.bfloat16)

    pl.semaphore_wait(barrier, groups + owners - 2)
    for k in range(chunks):
        near_copy(feats[k // per_layer], k, core).start()

    def stream_copy(way, k):
        return pltpu.make_async_remote_copy(
            src_ref=lines.at[k, way],
            dst_ref=lines.at[k, way],
            send_sem=hop_send.at[way, k],
            recv_sem=hop_recv.at[way, k],
            device_id={"grp": (me + 2, me - 2)[way]},
            device_id_type=mesh_id,
        )

    def passes_on(way):
        return (chip < last, chip > 0)[way]

    def here(k):
        return tokens_in[k].reshape(raw, chunk)

    def mine(way, k):
        return jnp.dot(slots[way], here(k), preferred_element_type=jnp.float32)

    def begin(way, k):
        lines[k, way] = mine(way, k).astype(jnp.bfloat16)
        stream_copy(way, k).start()

    def relay(way, k):
        stream_copy(way, k).wait_recv()
        lines[k, way] = (lines[k, way].astype(jnp.float32) + mine(way, k)).astype(jnp.bfloat16)
        stream_copy(way, k).start()

    def lead(position, k):
        for way in range(2):
            @pl.when(chip == (position, last - position)[way])
            def _():
                own_read(feats[k // per_layer], k).wait()
                near_copy(feats[k // per_layer], k, 1 - core).wait_recv()
                if position == 0:
                    begin(way, k)
                else:
                    relay(way, k)

    def pair_copy(k):
        return pltpu.make_async_remote_copy(
            src_ref=joined.at[0, k],
            dst_ref=joined.at[1, k],
            send_sem=pair_send.at[k],
            recv_sem=pair_recv.at[k],
            device_id={"grp": sibling},
            device_id_type=mesh_id,
        )

    def follow(k):
        for way in range(2):
            @pl.when(chip == (last, 0)[way])
            def _():
                stream_copy(way, k).wait_recv()

            @pl.when((chip < last) & (chip >= chips // 2) if way == 0 else (chip > 0) & (chip < chips // 2))
            def _():
                relay(way, k)

        seen = jnp.concatenate([lines[k, 0], here(k), lines[k, 1]], axis=0)
        joined[0, k] = jnp.dot(place[...], seen, preferred_element_type=jnp.float32).astype(
            jnp.bfloat16
        )
        pair_copy(k).start()

    diagonal = lax.broadcasted_iota(jnp.int32, (room, 128), 0) == lax.broadcasted_iota(
        jnp.int32, (room, 128), 1
    )

    def to_lanes(column):
        lanes = jnp.sum(jnp.where(diagonal, column, 0.0), axis=0, keepdims=True)
        return jnp.broadcast_to(lanes, (8, 128))

    def to_column(lanes):
        return jnp.sum(jnp.where(diagonal, lanes[0:1], 0.0), axis=1, keepdims=True)

    def part_copy(d, h):
        return pltpu.make_async_remote_copy(
            src_ref=coded.at[d - 1, h],
            dst_ref=arrived.at[d - 1, h],
            send_sem=part_send.at[d - 1, h, 0],
            recv_sem=part_recv.at[d - 1, h, 0],
            device_id={"tp": lax.rem(own + d, owners)},
            device_id_type=mesh_id,
        )

    def scale_copy(d, h):
        return pltpu.make_async_remote_copy(
            src_ref=scales.at[d - 1, h],
            dst_ref=scales_in.at[d - 1, h],
            send_sem=part_send.at[d - 1, h, 1],
            recv_sem=part_recv.at[d - 1, h, 1],
            device_id={"tp": lax.rem(own + d, owners)},
            device_id_type=mesh_id,
        )

    def send_part(d, h):
        target = lax.rem(own + d, owners)
        block = sums[h, pl.ds(pl.multiple_of(target * room, 8), room), :]
        top = jnp.maximum(jnp.max(jnp.abs(block), axis=1, keepdims=True), 1e-30)
        code = jnp.round(block * (LEVELS / top))
        code = jnp.concatenate([code[:, : piece // 2], code[:, piece // 2 :]], axis=0)
        coded[d - 1, h] = code.astype(jnp.int32).astype(jnp.int16)
        scales[d - 1, h] = to_lanes(top / LEVELS)
        part_copy(d, h).start()
        scale_copy(d, h).start()

    def take_part(d, h):
        part_copy(d, h).wait_recv()
        scale_copy(d, h).wait_recv()
        code = arrived[d - 1, h].astype(jnp.int32).astype(jnp.float32)
        code = jnp.concatenate([code[:room], code[room:]], axis=1)
        return code * to_column(scales_in[d - 1, h])

    def multiply(k, first, final):
        for side in range(2):
            weight_copy(k, side).wait()
        pair_copy(k).wait_recv()

        def columns_of(h):
            cols = pl.ds(pl.multiple_of(h * piece, piece), piece)

            def product(side):
                return jnp.dot(
                    joined[side, k], weights[k, side, :, cols], preferred_element_type=jnp.float32
                )

            value = product(0) + product(1)
            if first:
                sums[h] = value
            else:
                sums[h] += value

        if final:
            for h in range(pieces):
                columns_of(h)
                for d in range(1, owners):
                    send_part(d, h)
        else:
            pl.loop(0, pieces)(columns_of)

    leads = [2 * (last - 2 * position) for position in range(chips // 2)]
    for position, a in enumerate(leads):
        for k in range(min(a, chunks)):
            lead(position, k)
    for k in range(chunks):
        for position, a in enumerate(leads):
            if k + a < chunks:
                lead(position, k + a)
        follow(k)
        if k > 0:
            multiply(k - 1, k == 1, False)
    multiply(chunks - 1, False, True)

    square = jnp.zeros((room, 1), jnp.float32)
    for h in range(pieces):
        whole = sums[h, pl.ds(pl.multiple_of(own * room, 8), room), :]
        for d in range(1, owners):
            whole = whole + take_part(d, h)
        kept[h] = whole
        square = square + jnp.sum(whole * whole, axis=1, keepdims=True)
    squares[0] = to_lanes(square)

    def square_copy(d):
        return pltpu.make_async_remote_copy(
            src_ref=squares.at[0],
            dst_ref=squares.at[d],
            send_sem=sq_send.at[d - 1],
            recv_sem=sq_recv.at[d - 1],
            device_id={"grp": lax.rem(me + d, groups)},
            device_id_type=mesh_id,
        )

    for d in range(1, groups):
        square_copy(d).start()
    for d in range(1, groups):
        square_copy(d).wait_recv()
    lanes = squares[0]
    for d in range(1, groups):
        lanes = lanes + squares[d]
    inverse = lax.rsqrt(to_column(lanes) / width + EPSILON)
    for h in range(pieces):
        cols = slice(h * piece, (h + 1) * piece)
        normed = (kept[h] * inverse * gain_ref[:, cols]).astype(jnp.bfloat16)
        out_ref[:, cols] = jnp.dot(
            spread[...], normed, preferred_element_type=jnp.float32
        ).astype(jnp.bfloat16)

    for k in range(chunks):
        for way in range(2):
            @pl.when(passes_on(way))
            def _():
                stream_copy(way, k).wait_send()

        pair_copy(k).wait_send()
    for k in range(chunks):
        near_copy(feats[k // per_layer], k, core).wait_send()
    for d in range(1, owners):
        for h in range(pieces):
            part_copy(d, h).wait_send()
            scale_copy(d, h).wait_send()
    for d in range(1, groups):
        square_copy(d).wait_send()


def fast_call(groups, owners, hop, room, collective_id, *args):
    tokens, depth = args[0].shape
    columns = args[3].shape[1]
    rows = args[7].shape[0]
    slab = rows * POS // owners
    half = depth // 2
    chunk = min(CHUNK, half)
    chunks = LAYERS * half // chunk
    piece = min(PIECE, columns)
    pieces = columns // piece
    wide = 2 * hop + 2 * tokens

    vmem = pl.BlockSpec(memory_space=pltpu.VMEM)
    hbm = pl.BlockSpec(memory_space=pl.ANY)
    smem = pl.BlockSpec(memory_space=pltpu.SMEM)
    dma = pltpu.SemaphoreType.DMA
    return pl.pallas_call(
        functools.partial(fast_kernel, groups, owners, hop, room),
        out_shape=jax.ShapeDtypeStruct((slab, columns), jnp.bfloat16),
        in_specs=[hbm] * 6 + [vmem] + [smem] * 2,
        out_specs=vmem,
        scratch_shapes=[
            pltpu.VMEM((chunks, 2, hop, chunk), jnp.bfloat16),
            pltpu.VMEM((chunks, 2, tokens, chunk), jnp.bfloat16),
            pltpu.VMEM((chunks, 2, chunk, columns), jnp.bfloat16),
            pltpu.VMEM((2, chunks, owners * room, chunk), jnp.bfloat16),
            pltpu.VMEM((pieces, owners * room, piece), jnp.float32),
            pltpu.VMEM((owners - 1, pieces, 2 * room, piece // 2), jnp.int16),
            pltpu.VMEM((owners - 1, pieces, 2 * room, piece // 2), jnp.int16),
            pltpu.VMEM((owners - 1, pieces, 8, 128), jnp.float32),
            pltpu.VMEM((owners - 1, pieces, 8, 128), jnp.float32),
            pltpu.VMEM((pieces, room, piece), jnp.float32),
            pltpu.VMEM((groups, 8, 128), jnp.float32),
            pltpu.VMEM((2, hop, 2 * tokens), jnp.bfloat16),
            pltpu.VMEM((owners * room, wide), jnp.bfloat16),
            pltpu.VMEM((slab, room), jnp.bfloat16),
            pltpu.SMEM((rows,), jnp.int32),
            dma((chunks,)),
            dma((chunks,)),
            dma((chunks,)),
            dma((chunks, 2)),
            dma((2, chunks)),
            dma((2, chunks)),
            dma((chunks,)),
            dma((chunks,)),
            dma((owners - 1, pieces, 2)),
            dma((owners - 1, pieces, 2)),
            dma((groups - 1,)),
            dma((groups - 1,)),
        ],
        compiler_params=pltpu.CompilerParams(
            collective_id=collective_id, has_side_effects=True, vmem_limit_bytes=67043328
        ),
    )(*args[:6], args[6][None, :], *args[7:])


def choose(sizes, owners, accepted_ref, assignment_ref, which_ref):
    rows = accepted_ref.shape[0]
    chip_rows = 2 * ROWS_G

    def add_row(r, carry):
        low, high = carry
        count = accepted_ref[r] + 1
        return low + jnp.where(r < chip_rows, 0, count), high + jnp.where(r < rows - chip_rows, count, 0)

    low, high = lax.fori_loop(0, rows, add_row, (jnp.int32(0), jnp.int32(0)), unroll=8)
    passed = jnp.maximum(low, high)

    def add_slot(j, carry):
        used, most = carry
        used = jnp.where(j % (rows // owners) == 0, 0, used) + accepted_ref[assignment_ref[j]] + 1
        return used, jnp.maximum(most, used)

    _, owned = lax.fori_loop(0, rows, add_slot, (jnp.int32(0), jnp.int32(0)), unroll=8)
    which = jnp.int32(0)
    for hop, room in sizes:
        which = which + jnp.where((passed > hop) | (owned > room), 1, 0)
    which_ref[0] = which


def per_device(groups, owners, *args):
    accepted, assignment = args[7:]
    rows = accepted.shape[0]
    slab = rows * POS // owners
    sizes = [(groups * CAPACITY * 7 // 16 // 16 * 16, slab * 5 // 12), (groups * CAPACITY // 2, slab // 2)]
    smem = pl.BlockSpec(memory_space=pltpu.SMEM)
    which = pl.pallas_call(
        functools.partial(choose, sizes, owners),
        out_shape=jax.ShapeDtypeStruct((1,), jnp.int32),
        in_specs=[smem] * 2,
        out_specs=smem,
    )(accepted, assignment)
    calls = [
        functools.partial(fast_call, groups, owners, hop, room, 1 + i)
        for i, (hop, room) in enumerate(sizes)
    ]
    return lax.switch(which[0], calls + [functools.partial(full_call, groups, owners)], *args)


def solution(mesh):
    in_specs = (
        P("grp", "tp"),
        P("grp", "tp"),
        P("grp", "tp"),
        P("tp", "grp"),
        P("tp", "grp"),
        P("tp", "grp"),
        P("grp"),
        P(),
        P(),
    )
    return jax.shard_map(
        functools.partial(per_device, mesh.shape["grp"], mesh.shape["tp"]),
        mesh=mesh,
        in_specs=in_specs,
        out_specs=P("tp", "grp"),
        check_vma=False,
    )
```

```python
import functools

import jax
import jax.numpy as jnp
from jax import lax
from jax.experimental import pallas as pl
from jax.experimental.pallas import tpu as pltpu
from jax.sharding import PartitionSpec as P

ROWS_G = 8
POS = 6
CAPACITY = 4 * ROWS_G
BATCHES = 2
SLOTS = CAPACITY // BATCHES
LAYERS = 3
STEPS = BATCHES * LAYERS
AHEAD = 2
TILE = 256
PIECES = 1
EPSILON = 1e-05


def kernel(
    groups, owners,
    low_ref, mid_ref, high_ref, w_low, w_mid, w_high, gain_ref, accepted_ref, assignment_ref,
    out_ref,
    feats, weights, blocks, sums, parts, squares, rows_out, pick,
    f_sem, w_sem, send_sem, recv_sem, part_send, part_recv, sq_send, sq_recv, row_send, row_recv,
):
    me = lax.axis_index("grp")
    own = lax.axis_index("tp")
    chip, core = me // 2, me % 2
    chips = groups // 2
    sibling = chip * 2 + 1 - core
    columns = sums.shape[2]
    share = rows_out.shape[2]
    width = groups * columns
    tiles = columns // TILE
    tokens = feats.shape[1]
    slab = out_ref.shape[0]
    pair_slots = 2 * CAPACITY // ROWS_G

    reads = [
        pltpu.make_async_copy(f, feats.at[i], f_sem.at[i])
        for i, f in enumerate((low_ref, mid_ref, high_ref))
    ]
    for read in reads:
        read.start()
    loads = [
        pltpu.make_async_copy(w, weights.at[i], w_sem.at[i])
        for i, w in enumerate((w_low, w_mid, w_high))
    ]

    barrier = pltpu.get_barrier_semaphore()
    for d in range(1, groups):
        pl.semaphore_signal(
            barrier, inc=1, device_id={"grp": lax.rem(me + d, groups)},
            device_id_type=pl.DeviceIdType.MESH,
        )
    for d in range(1, owners):
        pl.semaphore_signal(
            barrier, inc=1, device_id={"tp": lax.rem(own + d, owners)},
            device_id_type=pl.DeviceIdType.MESH,
        )

    def rows_of(group):
        return pl.ds(pl.multiple_of(group * SLOTS, SLOTS), SLOTS)

    slot = lax.broadcasted_iota(jnp.int32, (CAPACITY, tokens), 0)
    token = lax.broadcasted_iota(jnp.int32, (CAPACITY, tokens), 1)
    packing = jnp.zeros((CAPACITY, tokens), jnp.float32)
    for k in range(ROWS_G):
        count = accepted_ref[me * ROWS_G + k] + 1
        start = (k // 2) * pair_slots
        if k % 2 == 1:
            start = start + accepted_ref[me * ROWS_G + k - 1] + 1
        position = token - k * POS
        hit = (position >= 0) & (position < count) & (slot == start + position)
        packing = jnp.where(hit, 1.0, packing)
    packing = packing.astype(jnp.bfloat16)

    def pack(layer):
        reads[layer].wait()
        packed = jnp.dot(packing, feats[layer], preferred_element_type=jnp.float32)
        for b in range(BATCHES):
            blocks[b * LAYERS + layer, rows_of(me), :] = packed[
                b * SLOTS : (b + 1) * SLOTS
            ].astype(jnp.bfloat16)

    pack(0)
    pl.semaphore_wait(barrier, groups + owners - 2)

    def block_copy(way, step, group):
        target = (chip * 2 + 2 + core, chip * 2 - 2 + core, sibling)[way]
        return pltpu.make_async_remote_copy(
            src_ref=blocks.at[step, rows_of(group), :],
            dst_ref=blocks.at[step, rows_of(group), :],
            send_sem=send_sem.at[way, step, group // 2],
            recv_sem=recv_sem.at[step, group],
            device_id={"grp": target},
            device_id_type=pl.DeviceIdType.MESH,
        )

    def send_own(step):
        @pl.when(chip < chips - 1)
        def _():
            block_copy(0, step, me).start()

        @pl.when(chip > 0)
        def _():
            block_copy(1, step, me).start()

        block_copy(2, step, me).start()

    def relay(step, d):
        @pl.when(chip - d >= 0)
        def _():
            group = me - 2 * d
            block_copy(0, step, group).wait_recv()

            @pl.when(chip < chips - 1)
            def _():
                block_copy(0, step, group).start()

            block_copy(2, step, group).start()

        @pl.when(chip + d <= chips - 1)
        def _():
            group = me + 2 * d
            block_copy(1, step, group).wait_recv()

            @pl.when(chip > 0)
            def _():
                block_copy(1, step, group).start()

            block_copy(2, step, group).start()

    def relays(step, first, last):
        @pl.loop(first, last)
        def _(d):
            relay(step, d)

    def arrive(step):
        for q in range(chips):
            block_copy(2, step, q * 2 + 1 - core).wait_recv()

    def multiply(step):
        b, layer = step // LAYERS, step % LAYERS

        @pl.loop(0, tiles)
        def _(j):
            cols = pl.ds(pl.multiple_of(j * TILE, TILE), TILE)
            product = jnp.dot(
                blocks[step], weights[layer, :, cols], preferred_element_type=jnp.float32
            )
            if layer == 0:
                sums[b, :, cols] = product
            else:
                sums[b, :, cols] += product
            if layer == LAYERS - 1:
                @pl.when(j % piece_tiles == piece_tiles - 1)
                def _():
                    for d in range(1, owners):
                        part_copy(b, d, j // piece_tiles).start()

            if step + 1 < STEPS:
                relays(
                    step + 1,
                    1 + (chips - 1) * j // tiles,
                    1 + (chips - 1) * (j + 1) // tiles,
                )
            if b > 0 and layer == 1:
                @pl.when(j == tiles // 2)
                def _():
                    reduce(b - 1)

    def share_of(owner):
        return pl.ds(pl.multiple_of(owner * share, share), share)

    piece = columns // PIECES
    piece_tiles = tiles // PIECES

    def part_copy(b, d, h):
        cols = pl.ds(pl.multiple_of(h * piece, piece), piece)
        target = lax.rem(own + d, owners)
        return pltpu.make_async_remote_copy(
            src_ref=sums.at[b, share_of(target), cols],
            dst_ref=parts.at[b, d - 1, :, cols],
            send_sem=part_send.at[b, d - 1, h],
            recv_sem=part_recv.at[b, d - 1, h],
            device_id={"tp": target},
            device_id_type=pl.DeviceIdType.MESH,
        )

    def square_copy(b, d):
        return pltpu.make_async_remote_copy(
            src_ref=squares.at[b, 0],
            dst_ref=squares.at[b, d],
            send_sem=sq_send.at[b, d - 1],
            recv_sem=sq_recv.at[b, d - 1],
            device_id={"grp": lax.rem(me + d, groups)},
            device_id_type=pl.DeviceIdType.MESH,
        )

    def row_copy(b, d):
        return pltpu.make_async_remote_copy(
            src_ref=rows_out.at[b, own],
            dst_ref=rows_out.at[b, own],
            send_sem=row_send.at[b, d - 1],
            recv_sem=row_recv.at[b, d - 1],
            device_id={"tp": lax.rem(own + d, owners)},
            device_id_type=pl.DeviceIdType.MESH,
        )

    diagonal = lax.broadcasted_iota(jnp.int32, (share, 128), 0) == lax.broadcasted_iota(
        jnp.int32, (share, 128), 1
    )

    def reduce(b):
        def body(h, square):
            cols = pl.ds(pl.multiple_of(h * piece, piece), piece)
            total = sums[b, share_of(own), cols]
            for d in range(1, owners):
                part_copy(b, d, h).wait_recv()
                total = total + parts[b, d - 1, :, cols]
            parts[b, owners - 1, :, cols] = total
            return square + jnp.sum(total * total, axis=1, keepdims=True)

        square = lax.fori_loop(0, PIECES, body, jnp.zeros((share, 1), jnp.float32))
        lanes = jnp.sum(jnp.where(diagonal, square, 0.0), axis=0, keepdims=True)
        squares[b, 0] = jnp.broadcast_to(lanes, (8, 128))
        for d in range(1, groups):
            square_copy(b, d).start()

    def finish(b):
        for d in range(1, groups):
            square_copy(b, d).wait_recv()
        lanes = squares[b, 0]
        for d in range(1, groups):
            lanes = lanes + squares[b, d]
        square = jnp.sum(jnp.where(diagonal, lanes[0:1], 0.0), axis=1, keepdims=True)
        inverse = lax.rsqrt(square / width + EPSILON)
        rows_out[b, own] = (parts[b, owners - 1] * inverse * gain_ref[...]).astype(jnp.bfloat16)
        for d in range(1, owners):
            row_copy(b, d).start()

    send_own(0)
    pack(1)
    send_own(1)
    for load in loads:
        load.start()
    pack(2)

    column = lax.broadcasted_iota(jnp.int32, pick.shape, 1)
    batch_rows = groups * SLOTS
    batch_bits, slot_bits = batch_rows.bit_length() - 1, SLOTS.bit_length() - 1
    group_of = lax.shift_right_logical(column & (batch_rows - 1), slot_bits)
    slot_of = lax.shift_right_logical(column, batch_bits) * SLOTS + (column & (SLOTS - 1))
    place = group_of * CAPACITY + slot_of
    line = lax.broadcasted_iota(jnp.int32, pick.shape, 0)
    picking = jnp.zeros(pick.shape, jnp.float32)
    for k in range(slab // POS):
        source = assignment_ref[own * (slab // POS) + k]
        count = accepted_ref[source] + 1
        local = source & (ROWS_G - 1)
        odd = local & 1
        before = (accepted_ref[jnp.maximum(source - 1, 0)] + 1) * odd
        start = (source - local) // ROWS_G * CAPACITY + (local - odd) // 2 * pair_slots + before
        position = line - k * POS
        hit = (position >= 0) & (position < count) & (place == start + position)
        picking = jnp.where(hit, 1.0, picking)
    pick[...] = picking.astype(jnp.bfloat16)

    relays(0, 1, chips)
    arrive(0)
    for step in range(STEPS):
        if step + AHEAD < STEPS:
            send_own(step + AHEAD)
        if step < LAYERS:
            loads[step].wait()
        multiply(step)
        if step + 1 < STEPS:
            arrive(step + 1)
        if step >= LAYERS and step % LAYERS == 2:
            finish(step // LAYERS - 1)
    reduce(BATCHES - 1)
    finish(BATCHES - 1)
    for b in range(BATCHES):
        for d in range(1, owners):
            row_copy(b, d).wait_recv()

    everything = rows_out[...].reshape(BATCHES * owners * share, columns)
    out_ref[...] = jnp.dot(
        pick[...], everything, preferred_element_type=jnp.float32
    ).astype(jnp.bfloat16)

    for step in range(STEPS):
        for q in range(chips):
            group = q * 2 + core

            @pl.when((chip < chips - 1) & (q <= chip))
            def _():
                block_copy(0, step, group).wait_send()

            @pl.when((chip > 0) & (q >= chip))
            def _():
                block_copy(1, step, group).wait_send()

            block_copy(2, step, group).wait_send()
    for b in range(BATCHES):
        for d in range(1, owners):
            for h in range(PIECES):
                part_copy(b, d, h).wait_send()
            row_copy(b, d).wait_send()
        for d in range(1, groups):
            square_copy(b, d).wait_send()


def full_call(
    groups, owners,
    low_feats, mid_feats, high_feats, w_low, w_mid, w_high, norm_gain, accepted, assignment,
):
    tokens, depth = low_feats.shape
    columns = w_low.shape[1]
    rows = accepted.shape[0]
    batch_rows = groups * SLOTS
    share = batch_rows // owners
    slab = rows * POS // owners

    vmem = pl.BlockSpec(memory_space=pltpu.VMEM)
    hbm = pl.BlockSpec(memory_space=pl.ANY)
    smem = pl.BlockSpec(memory_space=pltpu.SMEM)
    dma = pltpu.SemaphoreType.DMA
    return pl.pallas_call(
        functools.partial(kernel, groups, owners),
        out_shape=jax.ShapeDtypeStruct((slab, columns), jnp.bfloat16),
        in_specs=[hbm] * 6 + [vmem] + [smem] * 2,
        out_specs=vmem,
        scratch_shapes=[
            pltpu.VMEM((LAYERS, tokens, depth), jnp.bfloat16),
            pltpu.VMEM((LAYERS, depth, columns), jnp.bfloat16),
            pltpu.VMEM((STEPS, batch_rows, depth), jnp.bfloat16),
            pltpu.VMEM((BATCHES, batch_rows, columns), jnp.float32),
            pltpu.VMEM((BATCHES, owners, share, columns), jnp.float32),
            pltpu.VMEM((BATCHES, groups, 8, 128), jnp.float32),
            pltpu.VMEM((BATCHES, owners, share, columns), jnp.bfloat16),
            pltpu.VMEM((slab, BATCHES * batch_rows), jnp.bfloat16),
            dma((LAYERS,)),
            dma((LAYERS,)),
            dma((3, STEPS, groups // 2)),
            dma((STEPS, groups)),
            dma((BATCHES, owners - 1, PIECES)),
            dma((BATCHES, owners - 1, PIECES)),
            dma((BATCHES, groups - 1)),
            dma((BATCHES, groups - 1)),
            dma((BATCHES, owners - 1)),
            dma((BATCHES, owners - 1)),
        ],
        compiler_params=pltpu.CompilerParams(
            collective_id=0, has_side_effects=True, vmem_limit_bytes=67043328
        ),
    )(low_feats, mid_feats, high_feats, w_low, w_mid, w_high, norm_gain[None, :], accepted, assignment)


CHUNK = 512
PIECE = 1024
LEVELS = 32767.0


def fast_kernel(
    groups, owners, hop, room,
    low_ref, mid_ref, high_ref, w_low, w_mid, w_high, gain_ref, accepted_ref, assignment_ref,
    out_ref,
    lines, firsts, tokens_in, weights, joined, sums, coded, arrived, scales, scales_in, kept, squares, slots, place, spread, before,
    raw_sem, near_sem, near_send, w_sem, hop_send, hop_recv, pair_send, pair_recv,
    part_send, part_recv, sq_send, sq_recv,
):
    me = lax.axis_index("grp")
    own = lax.axis_index("tp")
    chip, core = me // 2, me % 2
    chips = groups // 2
    last = chips - 1
    sibling = chip * 2 + 1 - core
    feats = (low_ref, mid_ref, high_ref)
    tokens, depth = low_ref.shape
    pieces, _, piece = sums.shape
    columns = pieces * piece
    half = depth // 2
    chunk = joined.shape[3]
    per_layer = half // chunk
    chunks = LAYERS * per_layer
    rows = accepted_ref.shape[0]
    slab = out_ref.shape[0]
    row_slots = slab // POS
    chip_rows = 2 * ROWS_G
    raw = 2 * tokens
    width = groups * columns
    mesh_id = pl.DeviceIdType.MESH

    barrier = pltpu.get_barrier_semaphore()
    for d in range(1, groups):
        pl.semaphore_signal(
            barrier, inc=1, device_id={"grp": lax.rem(me + d, groups)}, device_id_type=mesh_id
        )
    for d in range(1, owners):
        pl.semaphore_signal(
            barrier, inc=1, device_id={"tp": lax.rem(own + d, owners)}, device_id_type=mesh_id
        )

    def feature_cols(which, part):
        return pl.ds(pl.multiple_of(which * half + part * chunk, chunk), chunk)

    def own_read(f, k):
        return pltpu.make_async_copy(
            f.at[:, feature_cols(core, k % per_layer)], tokens_in.at[k, core], raw_sem.at[k]
        )

    def near_copy(f, k, side):
        return pltpu.make_async_remote_copy(
            src_ref=f.at[:, feature_cols(1 - core, k % per_layer)],
            dst_ref=tokens_in.at[k, side],
            send_sem=near_send.at[k],
            recv_sem=near_sem.at[k],
            device_id={"grp": sibling},
            device_id_type=mesh_id,
        )

    for k in range(chunks):
        own_read(feats[k // per_layer], k).start()

    def weight_copy(k, side):
        which = core + side - 2 * core * side
        at = pl.ds(pl.multiple_of(which * half + k % per_layer * chunk, chunk), chunk)
        return pltpu.make_async_copy(
            (w_low, w_mid, w_high)[k // per_layer].at[at, :], weights.at[k, side], w_sem.at[k, side]
        )

    for k in range(chunks):
        for side in range(2):
            weight_copy(k, side).start()

    def count_row(r, total):
        before[r] = total
        return total + accepted_ref[r] + 1

    total = lax.fori_loop(0, rows, count_row, jnp.int32(0))

    token = lax.broadcasted_iota(jnp.int32, (1, raw), 1)
    slot = jnp.full((1, raw), -1, jnp.int32)
    for k in range(chip_rows):
        r = chip * chip_rows + k
        position = token - k * POS
        hit = (position >= 0) & (position <= accepted_ref[r])
        slot = jnp.where(hit, before[r] + position, slot)
    line = lax.broadcasted_iota(jnp.int32, (hop, raw), 0)
    slots[0] = jnp.where(line == slot, 1.0, 0.0).astype(jnp.bfloat16)
    from_end = jnp.where(slot >= 0, slot + (hop - total), -1)
    slots[1] = jnp.where(line == from_end, 1.0, 0.0).astype(jnp.bfloat16)

    lane = lax.broadcasted_iota(jnp.int32, (1, 2 * hop + raw), 1)

    def place_row(j, carry):
        dest, used = carry
        used = jnp.where(j % row_slots == 0, 0, used)
        r = assignment_ref[j]
        first = before[r]
        local = r - chip * chip_rows
        start = jnp.where(
            local < 0,
            first,
            jnp.where(local < chip_rows, hop + local * POS, hop + raw + hop - total + first),
        )
        position = lane - start
        hit = (position >= 0) & (position <= accepted_ref[r])
        dest = jnp.where(hit, j // row_slots * room + used + position, dest)
        return dest, used + accepted_ref[r] + 1

    dest, _ = lax.fori_loop(
        0, rows, place_row, (jnp.full(lane.shape, -1, jnp.int32), jnp.int32(0))
    )
    line = lax.broadcasted_iota(jnp.int32, place.shape, 0)
    place[...] = jnp.where(line == dest, 1.0, 0.0).astype(jnp.bfloat16)

    line = lax.broadcasted_iota(jnp.int32, spread.shape, 0)
    column = lax.broadcasted_iota(jnp.int32, spread.shape, 1)
    spreading = jnp.zeros(spread.shape, jnp.float32)
    used = jnp.int32(0)
    for k in range(row_slots):
        more = accepted_ref[assignment_ref[own * row_slots + k]]
        position = line - k * POS
        hit = (position >= 0) & (position <= more) & (column == used + position)
        spreading = jnp.where(hit, 1.0, spreading)
        used = used + more + 1
    spread[...] = spreading.astype(jnp.bfloat16)

    pl.semaphore_wait(barrier, groups + owners - 2)
    for k in range(chunks):
        near_copy(feats[k // per_layer], k, core).start()

    def stream_copy(way, k):
        return pltpu.make_async_remote_copy(
            src_ref=lines.at[k, way],
            dst_ref=lines.at[k, way],
            send_sem=hop_send.at[way, k],
            recv_sem=hop_recv.at[way, k],
            device_id={"grp": (me + 2, me - 2)[way]},
            device_id_type=mesh_id,
        )

    def here(k):
        return tokens_in[k].reshape(raw, chunk)

    def mine(way, k):
        return jnp.dot(slots[way], here(k), preferred_element_type=jnp.float32)

    first = firsts.shape[1]

    def first_copy(way, k):
        return pltpu.make_async_remote_copy(
            src_ref=firsts.at[k],
            dst_ref=firsts.at[k],
            send_sem=hop_send.at[way, k],
            recv_sem=hop_recv.at[way, k],
            device_id={"grp": (me + 2, me - 2)[way]},
            device_id_type=mesh_id,
        )

    def begin(way, k):
        packed = mine(way, k).astype(jnp.bfloat16)
        firsts[k] = (packed[:first], packed[hop - first :])[way]
        first_copy(way, k).start()
        lines[k, way] = packed

    def relay_first(way, k):
        first_copy(way, k).wait_recv()
        packed, came = mine(way, k), firsts[k].astype(jnp.float32)
        if way == 0:
            packed = jnp.concatenate([packed[:first] + came, packed[first:]], axis=0)
        else:
            packed = jnp.concatenate([packed[: hop - first], packed[hop - first :] + came], axis=0)
        lines[k, way] = packed.astype(jnp.bfloat16)
        stream_copy(way, k).start()

    def relay(way, k):
        stream_copy(way, k).wait_recv()
        lines[k, way] = (lines[k, way].astype(jnp.float32) + mine(way, k)).astype(jnp.bfloat16)
        stream_copy(way, k).start()

    def lead(position, k):
        for way in range(2):
            @pl.when(chip == (position, last - position)[way])
            def _():
                own_read(feats[k // per_layer], k).wait()
                near_copy(feats[k // per_layer], k, 1 - core).wait_recv()
                if position == 0:
                    begin(way, k)
                elif position == 1:
                    relay_first(way, k)
                else:
                    relay(way, k)

    def pair_copy(k):
        return pltpu.make_async_remote_copy(
            src_ref=joined.at[0, k],
            dst_ref=joined.at[1, k],
            send_sem=pair_send.at[k],
            recv_sem=pair_recv.at[k],
            device_id={"grp": sibling},
            device_id_type=mesh_id,
        )

    def follow(k):
        for way in range(2):
            @pl.when(chip == (last, 0)[way])
            def _():
                stream_copy(way, k).wait_recv()

            @pl.when((chip < last) & (chip >= chips // 2) if way == 0 else (chip > 0) & (chip < chips // 2))
            def _():
                relay(way, k)

        seen = jnp.concatenate([lines[k, 0], here(k), lines[k, 1]], axis=0)
        joined[0, k] = jnp.dot(place[...], seen, preferred_element_type=jnp.float32).astype(
            jnp.bfloat16
        )
        pair_copy(k).start()

    diagonal = lax.broadcasted_iota(jnp.int32, (room, 128), 0) == lax.broadcasted_iota(
        jnp.int32, (room, 128), 1
    )

    def to_lanes(column):
        lanes = jnp.sum(jnp.where(diagonal, column, 0.0), axis=0, keepdims=True)
        return jnp.broadcast_to(lanes, (8, 128))

    def to_column(lanes):
        return jnp.sum(jnp.where(diagonal, lanes[0:1], 0.0), axis=1, keepdims=True)

    def part_copy(d, h):
        return pltpu.make_async_remote_copy(
            src_ref=coded.at[d - 1, h],
            dst_ref=arrived.at[d - 1, h],
            send_sem=part_send.at[d - 1, h, 0],
            recv_sem=part_recv.at[d - 1, h, 0],
            device_id={"tp": lax.rem(own + d, owners)},
            device_id_type=mesh_id,
        )

    def scale_copy(d, h):
        return pltpu.make_async_remote_copy(
            src_ref=scales.at[d - 1, h],
            dst_ref=scales_in.at[d - 1, h],
            send_sem=part_send.at[d - 1, h, 1],
            recv_sem=part_recv.at[d - 1, h, 1],
            device_id={"tp": lax.rem(own + d, owners)},
            device_id_type=mesh_id,
        )

    def send_part(d, h):
        target = lax.rem(own + d, owners)
        block = sums[h, pl.ds(pl.multiple_of(target * room, 8), room), :]
        top = jnp.maximum(jnp.max(jnp.abs(block), axis=1, keepdims=True), 1e-30)
        code = jnp.round(block * (LEVELS / top))
        code = jnp.concatenate([code[:, : piece // 2], code[:, piece // 2 :]], axis=0)
        coded[d - 1, h] = code.astype(jnp.int32).astype(jnp.int16)
        scales[d - 1, h] = to_lanes(top / LEVELS)
        part_copy(d, h).start()
        scale_copy(d, h).start()

    def take_part(d, h):
        part_copy(d, h).wait_recv()
        scale_copy(d, h).wait_recv()
        code = arrived[d - 1, h].astype(jnp.int32).astype(jnp.float32)
        code = jnp.concatenate([code[:room], code[room:]], axis=1)
        return code * to_column(scales_in[d - 1, h])

    def multiply(k, first, final):
        for side in range(2):
            weight_copy(k, side).wait()
        pair_copy(k).wait_recv()

        def columns_of(h):
            cols = pl.ds(pl.multiple_of(h * piece, piece), piece)

            def product(side):
                return jnp.dot(
                    joined[side, k], weights[k, side, :, cols], preferred_element_type=jnp.float32
                )

            value = product(0) + product(1)
            if first:
                sums[h] = value
            else:
                sums[h] += value

        if final:
            for h in range(pieces):
                columns_of(h)
                for d in range(1, owners):
                    send_part(d, h)
        else:
            pl.loop(0, pieces)(columns_of)

    leads = [2 * (last - 2 * position) for position in range(chips // 2)]
    for position, a in enumerate(leads):
        for k in range(min(a, chunks)):
            lead(position, k)
    for k in range(chunks):
        for position, a in enumerate(leads):
            if k + a < chunks:
                lead(position, k + a)
        follow(k)
        if k > 0:
            multiply(k - 1, k == 1, False)
    multiply(chunks - 1, False, True)

    square = jnp.zeros((room, 1), jnp.float32)
    for h in range(pieces):
        whole = sums[h, pl.ds(pl.multiple_of(own * room, 8), room), :]
        for d in range(1, owners):
            whole = whole + take_part(d, h)
        kept[h] = whole
        square = square + jnp.sum(whole * whole, axis=1, keepdims=True)
    squares[0] = to_lanes(square)

    def square_copy(d):
        return pltpu.make_async_remote_copy(
            src_ref=squares.at[0],
            dst_ref=squares.at[d],
            send_sem=sq_send.at[d - 1],
            recv_sem=sq_recv.at[d - 1],
            device_id={"grp": lax.rem(me + d, groups)},
            device_id_type=mesh_id,
        )

    for d in range(1, groups):
        square_copy(d).start()
    for d in range(1, groups):
        square_copy(d).wait_recv()
    lanes = squares[0]
    for d in range(1, groups):
        lanes = lanes + squares[d]
    inverse = lax.rsqrt(to_column(lanes) / width + EPSILON)
    for h in range(pieces):
        cols = slice(h * piece, (h + 1) * piece)
        normed = (kept[h] * inverse * gain_ref[:, cols]).astype(jnp.bfloat16)
        out_ref[:, cols] = jnp.dot(
            spread[...], normed, preferred_element_type=jnp.float32
        ).astype(jnp.bfloat16)

    for k in range(chunks):
        for way in range(2):
            @pl.when(chip == (0, last)[way])
            def _():
                first_copy(way, k).wait_send()

            @pl.when((chip > 0) & (chip < last))
            def _():
                stream_copy(way, k).wait_send()

        pair_copy(k).wait_send()
    for k in range(chunks):
        near_copy(feats[k // per_layer], k, core).wait_send()
    for d in range(1, owners):
        for h in range(pieces):
            part_copy(d, h).wait_send()
            scale_copy(d, h).wait_send()
    for d in range(1, groups):
        square_copy(d).wait_send()


def fast_call(groups, owners, hop, room, collective_id, *args):
    tokens, depth = args[0].shape
    columns = args[3].shape[1]
    rows = args[7].shape[0]
    slab = rows * POS // owners
    half = depth // 2
    chunk = min(CHUNK, half)
    chunks = LAYERS * half // chunk
    piece = min(PIECE, columns)
    pieces = columns // piece
    wide = 2 * hop + 2 * tokens

    vmem = pl.BlockSpec(memory_space=pltpu.VMEM)
    hbm = pl.BlockSpec(memory_space=pl.ANY)
    smem = pl.BlockSpec(memory_space=pltpu.SMEM)
    dma = pltpu.SemaphoreType.DMA
    return pl.pallas_call(
        functools.partial(fast_kernel, groups, owners, hop, room),
        out_shape=jax.ShapeDtypeStruct((slab, columns), jnp.bfloat16),
        in_specs=[hbm] * 6 + [vmem] + [smem] * 2,
        out_specs=vmem,
        scratch_shapes=[
            pltpu.VMEM((chunks, 2, hop, chunk), jnp.bfloat16),
            pltpu.VMEM((chunks, 2 * CAPACITY, chunk), jnp.bfloat16),
            pltpu.VMEM((chunks, 2, tokens, chunk), jnp.bfloat16),
            pltpu.VMEM((chunks, 2, chunk, columns), jnp.bfloat16),
            pltpu.VMEM((2, chunks, owners * room, chunk), jnp.bfloat16),
            pltpu.VMEM((pieces, owners * room, piece), jnp.float32),
            pltpu.VMEM((owners - 1, pieces, 2 * room, piece // 2), jnp.int16),
            pltpu.VMEM((owners - 1, pieces, 2 * room, piece // 2), jnp.int16),
            pltpu.VMEM((owners - 1, pieces, 8, 128), jnp.float32),
            pltpu.VMEM((owners - 1, pieces, 8, 128), jnp.float32),
            pltpu.VMEM((pieces, room, piece), jnp.float32),
            pltpu.VMEM((groups, 8, 128), jnp.float32),
            pltpu.VMEM((2, hop, 2 * tokens), jnp.bfloat16),
            pltpu.VMEM((owners * room, wide), jnp.bfloat16),
            pltpu.VMEM((slab, room), jnp.bfloat16),
            pltpu.SMEM((rows,), jnp.int32),
            dma((chunks,)),
            dma((chunks,)),
            dma((chunks,)),
            dma((chunks, 2)),
            dma((2, chunks)),
            dma((2, chunks)),
            dma((chunks,)),
            dma((chunks,)),
            dma((owners - 1, pieces, 2)),
            dma((owners - 1, pieces, 2)),
            dma((groups - 1,)),
            dma((groups - 1,)),
        ],
        compiler_params=pltpu.CompilerParams(
            collective_id=collective_id, has_side_effects=True, vmem_limit_bytes=67043328
        ),
    )(*args[:6], args[6][None, :], *args[7:])


def choose(sizes, owners, accepted_ref, assignment_ref, which_ref):
    rows = accepted_ref.shape[0]
    chip_rows = 2 * ROWS_G

    def add_row(r, carry):
        low, high = carry
        count = accepted_ref[r] + 1
        return low + jnp.where(r < chip_rows, 0, count), high + jnp.where(r < rows - chip_rows, count, 0)

    low, high = lax.fori_loop(0, rows, add_row, (jnp.int32(0), jnp.int32(0)), unroll=8)
    passed = jnp.maximum(low, high)

    def add_slot(j, carry):
        used, most = carry
        used = jnp.where(j % (rows // owners) == 0, 0, used) + accepted_ref[assignment_ref[j]] + 1
        return used, jnp.maximum(most, used)

    _, owned = lax.fori_loop(0, rows, add_slot, (jnp.int32(0), jnp.int32(0)), unroll=8)
    which = jnp.int32(0)
    for hop, room in sizes:
        which = which + jnp.where((passed > hop) | (owned > room), 1, 0)
    which_ref[0] = which


def per_device(groups, owners, *args):
    accepted, assignment = args[7:]
    rows = accepted.shape[0]
    slab = rows * POS // owners
    six, seven, eight = (groups * CAPACITY * part // 16 // 16 * 16 for part in (6, 7, 8))
    small, large = slab * 5 // 12, slab // 2
    sizes = [(six, small), (seven, small), (seven, large), (eight, large)]
    smem = pl.BlockSpec(memory_space=pltpu.SMEM)
    which = pl.pallas_call(
        functools.partial(choose, sizes, owners),
        out_shape=jax.ShapeDtypeStruct((1,), jnp.int32),
        in_specs=[smem] * 2,
        out_specs=smem,
    )(accepted, assignment)
    calls = [
        functools.partial(fast_call, groups, owners, hop, room, 1 + i)
        for i, (hop, room) in enumerate(sizes)
    ]
    return lax.switch(which[0], calls + [functools.partial(full_call, groups, owners)], *args)


def solution(mesh):
    in_specs = (
        P("grp", "tp"),
        P("grp", "tp"),
        P("grp", "tp"),
        P("tp", "grp"),
        P("tp", "grp"),
        P("tp", "grp"),
        P("grp"),
        P(),
        P(),
    )
    return jax.shard_map(
        functools.partial(per_device, mesh.shape["grp"], mesh.shape["tp"]),
        mesh=mesh,
        in_specs=in_specs,
        out_specs=P("tp", "grp"),
        check_vma=False,
    )
```
